128 devices in a mesh: section: 2 (over core), vocab: 64 (over x, z, y).
Axes of the slice: x: 4, y: 4, z: 4, core: 2. Of those that a mesh axis runs over, the one named last changes fastest.
Arguments:
- hidden_in: bfloat16 [2, 256, 7168], P(None, ('section', 'vocab')), may hold values from -6 to 6
- gain_ffn: float32 [7168], replicated, may hold values from 0.4 to 1.6
- w_gate: bfloat16 [7168, 18432], P(None, ('section', 'vocab')), may hold values from -0.0625 to 0.0625
- w_up: bfloat16 [7168, 18432], P(None, ('section', 'vocab')), may hold values from -0.0625 to 0.0625
- w_down: bfloat16 [18432, 7168], P(('section', 'vocab')), may hold values from -0.046875 to 0.046875
- gain_final: float32 [7168], replicated, may hold values from 0.4 to 1.6
- head_weight: bfloat16 [7168, 129280], P(None, ('section', 'vocab')), may hold values from -4.5 to 4.5
- sampled_ids: int32 [2, 256], replicated, may hold values from 0 to 129279
- seq_ids: int32 [2, 256], P(None, ('section', 'vocab')), may hold values from 0 to 7, never falling along the last dimension, each value on 1 to 128 neighbouring positions
Outputs:
- token_logprob: float32 [2, 256], P(None, ('section', 'vocab'))
- log_norm: float32 [2, 256], P(None, ('section', 'vocab'))
- top_mass: float32 [2, 256], P(None, ('section', 'vocab'))
- seq_logprob: float32 [2, 8], replicated
The draws below stay inside these ranges and needn't reach their ends.
All inputs are finite; a program needn't handle non-finite values.
Results may differ from the reference program's by a relative error of at most 0.006.
Values may be sent and summed in bfloat16 or wider, within the bound.
A program may use at most 192 MiB of HBM per device.

```python
import math
import jax
import jax.numpy as jnp
import numpy as np
from jax import lax

D = 7168
FF = 18432
VOCAB = 129280
MB = 2
MB_TOK = 256
SEQS = 8
TOPK = 20


def draw_head_weight(key, part):
    base_key = jax.random.fold_in(key, 11)
    key_scale, key_entries = jax.random.split(base_key, 2)
    column_scale = jnp.exp(jax.random.uniform(key_scale, (1, VOCAB), jnp.float32, math.log(0.7), math.log(7.0)))
    entries = jax.random.normal(key_entries, (D, VOCAB), jnp.float32)
    weight = entries * column_scale / math.sqrt(D)
    return jnp.clip(weight, -4.5, 4.5).astype(jnp.bfloat16)


def place_ends(array, stream_key, least, top_value):
    extent = array.shape
    spot = [jax.random.randint(jax.random.fold_in(stream_key, axis), (), 0, extent[axis]) for axis in range(len(extent))]
    array = array.at[tuple(spot)].set(least)
    longest = extent.index(max(extent))
    spot[longest] = (spot[longest] + 1) % extent[longest]
    return array.at[tuple(spot)].set(top_value)


def steps_of(rng, extent, shards, least, high):
    gain, own = 1.0, jax.random.fold_in(rng, 6)
    for position, blocks in shards:
        draws = jnp.exp(jax.random.uniform(jax.random.fold_in(own, position), (blocks,), jnp.float32, least / len(shards), high / len(shards)))
        gain = gain * jnp.repeat(draws, extent[position] // blocks).reshape([-1 if axis == position else 1 for axis in range(len(extent))])
    return gain


def split_up(number_of, total, limit, skew):
    weights = [(1 << 20) // math.isqrt(rank ** skew) + 1 for rank in range(2, number_of + 1)]
    surplus, counts = total - limit - (number_of - 1), [1] * (number_of - 1)
    while surplus > 0:
        candidates = [i for i in range(number_of - 1) if counts[i] < limit]
        pool, left = sum([weights[i] for i in candidates]), surplus
        for i in candidates:
            more = min(limit - counts[i], max(1, left * weights[i] // pool), surplus)
            counts[i] = counts[i] + more
            surplus = surplus - more
    return np.array([limit] + counts)


def ragged_sizes(key, number_of, total, most, slope):
    if number_of == 2:
        one = jax.random.randint(key, (), max(1, total - most), min(most, total - 1) + 1)
        return jnp.stack([one, total - one])
    lengths = jnp.asarray(split_up(number_of, total, most, slope), jnp.int32)
    couples = (number_of - 1) // 2
    donor, taker = lengths[1:1 + 2 * couples:2], lengths[2:2 + 2 * couples:2]
    margin = jnp.minimum(donor - 1, most - taker)
    passed = jax.random.randint(jax.random.fold_in(key, 1), (couples,), 0, 1 << 20) % (margin + 1)
    lengths = lengths.at[1:1 + 2 * couples:2].set(donor - passed).at[2:2 + 2 * couples:2].set(taker + passed)
    return lengths[jax.random.permutation(jax.random.fold_in(key, 2), number_of)]


def gaussian(own_key, extent, width, limit, cuts=(), kind=jnp.bfloat16):
    values = jax.random.normal(own_key, extent, jnp.float32) * width
    if len(cuts) > 0:
        values = steps_of(own_key, extent, cuts, -0.22, 0.18) * values
    return jnp.clip(values, min=-limit, max=limit).astype(kind)


def setup_inputs(seed: int = 0) -> dict:
    streams_of = jax.random.split(jax.random.key(seed), 10)
    hidden_in = gaussian(streams_of[0], (MB, MB_TOK, D), 1.0, 6.0, ((1, 128),))
    gain_ffn = jnp.clip(1.0 + 0.12 * jax.random.normal(streams_of[1], (D,), jnp.float32), 0.4, 1.6)
    w_gate = gaussian(streams_of[2], (D, FF), D ** -0.5, 0.0625, ((1, 128),))
    w_up = gaussian(streams_of[3], (D, FF), D ** -0.5, 0.0625, ((1, 128),))
    w_down = gaussian(streams_of[4], (FF, D), FF ** -0.5, 0.046875, ((0, 128),))
    gain_final = jnp.clip(1.0 + 0.12 * jax.random.normal(streams_of[5], (D,), jnp.float32), 0.4, 1.6)
    head_weight = draw_head_weight(jax.random.fold_in(streams_of[9], 71), 0)
    sampled_ids = place_ends(jax.random.randint(streams_of[7], (MB, MB_TOK), 0, VOCAB), jax.random.fold_in(streams_of[7], 1), 0, VOCAB - 1).astype(jnp.int32)
    seq_ids = jax.vmap(lambda own: jnp.searchsorted(jnp.cumsum(ragged_sizes(own, SEQS, MB_TOK, MB_TOK // 2, 2)), jnp.arange(MB_TOK), side="right"))(jax.random.split(streams_of[8], MB)).reshape((MB, MB_TOK)).astype(jnp.int32)
    return {"hidden_in": hidden_in, "gain_ffn": gain_ffn, "w_gate": w_gate, "w_up": w_up, "w_down": w_down, "gain_final": gain_final, "head_weight": head_weight, "sampled_ids": sampled_ids, "seq_ids": seq_ids}


epsilon = 1e-06

def rms_norm(values, scale_gain):
    wide = values.astype(jnp.float32)
    square_mean = lax.optimization_barrier(jnp.mean(wide * wide, axis=-1, keepdims=True))
    return (wide * lax.rsqrt(square_mean + epsilon) * scale_gain).astype(jnp.bfloat16)

def largest(values):
    return lax.sort(values, dimension=values.ndim - 1)[..., -TOPK:]

def reference(hidden_in, gain_ffn, w_gate, w_up, w_down, gain_final, head_weight, sampled_ids, seq_ids):

    def score_batch(record):
        states, token_ids, segment_ids = record
        normed = rms_norm(states, gain_ffn)
        gate_proj = jnp.dot(normed, w_gate, preferred_element_type=jnp.float32)
        up_proj = jnp.dot(normed, w_up, preferred_element_type=jnp.float32)
        hidden_act = (jax.nn.silu(gate_proj) * up_proj).astype(jnp.bfloat16)
        branch = jnp.dot(hidden_act, w_down, preferred_element_type=jnp.float32)
        residual = (states.astype(jnp.float32) + branch).astype(jnp.bfloat16)
        scaled = rms_norm(residual, gain_final)
        logits = jnp.dot(scaled, head_weight, preferred_element_type=jnp.float32)
        peak_value = lax.optimization_barrier(jnp.max(logits, axis=1))
        log_norm = peak_value + jnp.log(lax.optimization_barrier(jnp.sum(jnp.exp(logits - peak_value[:, None]), axis=1)))
        sampled_logit = jnp.take_along_axis(logits, token_ids[:, None].astype(jnp.int32), axis=1)[:, 0]
        token_logprob = sampled_logit - log_norm
        leaders = largest(logits)
        top_mass = lax.optimization_barrier(jnp.sum(jnp.exp(leaders - log_norm[:, None]), axis=1))
        onehot = (segment_ids[:, None] == jnp.arange(SEQS, dtype=jnp.int32)[None, :]).astype(jnp.float32)
        seq_total = lax.optimization_barrier(jnp.sum(token_logprob[:, None] * onehot, axis=0))
        return (token_logprob, log_norm, top_mass, seq_total)
    token_logprob, log_norm, top_mass, seq_logprob = lax.map(score_batch, (hidden_in, sampled_ids, seq_ids))
    return (token_logprob, log_norm, top_mass, seq_logprob)
```

```python
import functools

import jax
import jax.numpy as jnp
from jax import lax
from jax.experimental import pallas as pl
from jax.experimental.pallas import tpu as pltpu
from jax.sharding import Mesh
from jax.sharding import PartitionSpec as P

SEQS = 8
TOPK = 20
EPS = 1e-06
NEG = -3.0e38
MESH = pl.DeviceIdType.MESH
CORE = "section"
AXES = ("x", "z", "y")
EVERY = (CORE,) + AXES
ORDERS = ((0, 1, 2), (1, 2, 0), (2, 0, 1))
N = 4


def pick(sel):
    return tuple(sel.get(i, slice(None)) for i in range(3))


def column_groups(width):
    tiles = width // 128
    cuts = [0, (tiles + 2) // 3, (2 * tiles + 2) // 3, tiles]
    return [pl.ds(128 * cuts[q], 128 * (cuts[q + 1] - cuts[q])) for q in range(3)]


def toward(axis, k):
    name = AXES[axis]
    return {name: lax.rem(lax.axis_index(name) + k, N)}


def partner():
    return {CORE: 1 - lax.axis_index(CORE)}


def meet():
    barrier = pltpu.get_barrier_semaphore()
    for axis in range(3):
        for k in (1, 2, 3):
            pl.semaphore_signal(barrier, inc=1, device_id=toward(axis, k), device_id_type=MESH)
    pl.semaphore_signal(barrier, inc=1, device_id=partner(), device_id_type=MESH)
    pl.semaphore_wait(barrier, 10)


class Mail:
    def __init__(self, send_sem, recv_sem):
        self.send_sem, self.recv_sem = send_sem, recv_sem
        self.copies, self.count = {}, 0

    def send(self, tag, src, dst, device):
        copy = pltpu.make_async_remote_copy(
            src_ref=src,
            dst_ref=dst,
            send_sem=self.send_sem.at[self.count],
            recv_sem=self.recv_sem.at[self.count],
            device_id=device,
            device_id_type=MESH,
        )
        copy.start()
        self.count += 1
        self.copies.setdefault(tag, []).append(copy)

    def received(self, tag):
        for copy in self.copies[tag]:
            copy.wait_recv()

    def all_sent(self):
        for copies in self.copies.values():
            for copy in copies:
                copy.wait_send()


def gather_start(buf, mail, groups):
    def go(q, tag, sel, axis):
        for k in (1, 3, 2):
            src, dst = dict(sel), dict(sel)
            src[axis], dst[axis] = 0, N - k
            rest = (slice(None), groups[q])
            mail.send((q, tag), buf.at[pick(src) + rest], buf.at[pick(dst) + rest], toward(axis, k))

    others = pl.ds(1, 3)
    for q, (a, b, c) in enumerate(ORDERS):
        go(q, "a", {b: 0, c: 0}, a)
    for q, (a, b, c) in enumerate(ORDERS):
        go(q, "b0", {a: 0, c: 0}, b)
    for q, (a, b, c) in enumerate(ORDERS):
        go(q, "c0", {a: 0, b: 0}, c)
    for q, (a, b, c) in enumerate(ORDERS):
        mail.received((q, "a"))
        go(q, "b1", {a: others, c: 0}, b)
    for q, (a, b, c) in enumerate(ORDERS):
        go(q, "c1", {a: others, b: 0}, c)
    for q, (a, b, c) in enumerate(ORDERS):
        mail.received((q, "b0"))
        go(q, "c2", {a: 0, b: others}, c)
    for q, (a, b, c) in enumerate(ORDERS):
        mail.received((q, "b1"))
        go(q, "c3", {a: others, b: others}, c)
    for tag in ("c0", "c1", "c2", "c3"):
        for q in range(3):
            mail.received((q, tag))


def settle(buf, out):
    @pl.loop(0, N)
    def _(i):
        @pl.loop(0, N)
        def _(j):
            for k in range(N):
                out[i * N + j, pl.ds(4 * k, 4), :] = buf[i, j, k]


def rms(wide, gain):
    mean = jnp.mean(wide * wide, axis=-1, keepdims=True)
    return (wide * lax.rsqrt(mean + EPS) * gain).astype(jnp.bfloat16)


def block_kernel(
    h_ref, gf_ref, gl_ref, wg_ref, wu_ref, wd_ref, hw_ref,
    x2_ref, hw2_ref,
    G, G2, X, S, R1, R2, R3, T1, T2, F, PB, W, WD, ACT,
    own_sem, swap_s, swap_r, g_s, g_r, r_s, r_r, g2_s, g2_r,
):
    groups = column_groups(h_ref.shape[-1])
    width = h_ref.shape[-1]
    loads = []
    for n, (src, dst) in enumerate(((wg_ref, W.at[0]), (wu_ref, W.at[1]), (wd_ref, WD.at[0]))):
        copy = pltpu.make_async_copy(src, dst, own_sem.at[n])
        copy.start()
        loads.append(copy)
    meet()
    G[0, 0, 0] = rms(h_ref[...].astype(jnp.float32), gf_ref[...])
    swap = Mail(swap_s, swap_r)
    for tag, src, dst in (("g", wg_ref, W.at[2]), ("u", wu_ref, W.at[3]), ("d", wd_ref, WD.at[1])):
        swap.send(tag, src, dst, partner())
    mail = Mail(g_s, g_r)
    gather_start(G, mail, groups)
    settle(G, X)
    for copy in loads:
        copy.wait()
    for tag in ("g", "u", "d"):
        swap.received(tag)
    swap.send("h", hw_ref, hw2_ref, partner())

    rows = N * N * N * 4
    hidden = W.shape[1]
    y = lax.dot_general(
        W[...].reshape(4 * hidden, width), X[...].reshape(rows, width), (((1,), (1,)), ((), ())),
        preferred_element_type=jnp.float32,
    )
    acts = []
    for p in range(2):
        gate, up = y[2 * p * hidden : (2 * p + 1) * hidden], y[(2 * p + 1) * hidden : (2 * p + 2) * hidden]
        acts.append(gate / (1.0 + jnp.exp(-gate)) * up)
    ACT[...] = jnp.concatenate(acts, axis=0).T.astype(jnp.bfloat16)
    step = PB.shape[-1]

    @pl.loop(0, width // step)
    def _(n):
        cols = pl.ds(pl.multiple_of(n * step, 128), step)
        down = WD[:, :, cols].reshape(2 * hidden, step)
        part = jnp.dot(ACT[...], down, preferred_element_type=jnp.float32)
        PB[...] = part.astype(jnp.bfloat16).reshape(PB.shape)
        for i in range(N):
            for j in range(N):
                for k in range(N):
                    S[i, j, k, :, cols] = PB[i * N + j, pl.ds(4 * k, 4), :]

    red = Mail(r_s, r_r)
    for k in (1, 3, 2):
        for q, (a, b, c) in enumerate(ORDERS):
            rest = (slice(None), groups[q])
            red.send((q, 1), S.at[pick({c: k}) + rest], R1.at[(k - 1, slice(None), slice(None)) + rest], toward(c, k))
    for q, (a, b, c) in enumerate(ORDERS):
        cols = groups[q]
        red.received((q, 1))

        @pl.loop(0, N)
        def _(i):
            @pl.loop(0, N)
            def _(j):
                left = [i, j]
                sel = {ax: left.pop(0) for ax in range(3) if ax != c}
                sel[c] = 0
                total = S[pick(sel) + (slice(None), cols)].astype(jnp.float32)
                for k in range(3):
                    total += R1[k, i, j, :, cols].astype(jnp.float32)
                T1[i, j, :, cols] = total.astype(jnp.bfloat16)

        first = min(a, b)
        for k in (1, 3, 2):
            src = T1.at[k, :, :, cols] if b == first else T1.at[:, k, :, cols]
            red.send((q, 2), src, R2.at[k - 1, :, :, cols], toward(b, k))
    for q, (a, b, c) in enumerate(ORDERS):
        cols = groups[q]
        red.received((q, 2))
        first = min(a, b)
        for i in range(N):
            total = (T1[0, i, :, cols] if b == first else T1[i, 0, :, cols]).astype(jnp.float32)
            for k in range(3):
                total += R2[k, i, :, cols].astype(jnp.float32)
            T2[i, :, cols] = total.astype(jnp.bfloat16)
        for k in (1, 3, 2):
            red.send((q, 3), T2.at[k, :, cols], R3.at[k - 1, :, cols], toward(a, k))
    for q in range(3):
        cols = groups[q]
        red.received((q, 3))
        total = T2[0, :, cols].astype(jnp.float32)
        for k in range(3):
            total += R3[k, :, cols].astype(jnp.float32)
        F[:, cols] = total

    residual = (h_ref[...].astype(jnp.float32) + F[...]).astype(jnp.bfloat16)
    G2[0, 0, 0] = rms(residual.astype(jnp.float32), gl_ref[...])
    mail2 = Mail(g2_s, g2_r)
    gather_start(G2, mail2, groups)
    settle(G2, x2_ref)
    swap.received("h")
    for m in (mail, swap, red, mail2):
        m.all_sent()


def dense_block(h, gain_ffn, gain_final, w_gate, w_up, w_down, head):
    hidden, width = w_gate.shape
    bf16, f32 = jnp.bfloat16, jnp.float32
    vmem, anywhere = pl.BlockSpec(memory_space=pltpu.VMEM), pl.BlockSpec(memory_space=pl.ANY)
    dma = lambda n: pltpu.SemaphoreType.DMA((n,))
    return pl.pallas_call(
        block_kernel,
        out_shape=(
            jax.ShapeDtypeStruct((N * N, N * 4, width), bf16),
            jax.ShapeDtypeStruct(head.shape, bf16),
        ),
        in_specs=[vmem, vmem, vmem, anywhere, anywhere, anywhere, anywhere],
        out_specs=(vmem, anywhere),
        scratch_shapes=[
            pltpu.VMEM((N, N, N, 4, width), bf16),
            pltpu.VMEM((N, N, N, 4, width), bf16),
            pltpu.VMEM((N * N, N * 4, width), bf16),
            pltpu.VMEM((N, N, N, 4, width), bf16),
            pltpu.VMEM((3, N, N, 4, width), bf16),
            pltpu.VMEM((3, N, 4, width), bf16),
            pltpu.VMEM((3, 4, width), bf16),
            pltpu.VMEM((N, N, 4, width), bf16),
            pltpu.VMEM((N, 4, width), bf16),
            pltpu.VMEM((4, width), f32),
            pltpu.VMEM((N * N, N * 4, 512), bf16),
            pltpu.VMEM((4, hidden, width), bf16),
            pltpu.VMEM((2, hidden, width), bf16),
            pltpu.VMEM((N**3 * 4, 2 * hidden), bf16),
            dma(3), dma(4), dma(4), dma(63), dma(63), dma(27), dma(27), dma(63), dma(63),
        ],
        compiler_params=pltpu.CompilerParams(collective_id=0, has_side_effects=True, vmem_limit_bytes=62 << 20),
        name="dense_block",
    )(h, gain_ffn, gain_final, w_gate, w_up, w_down, head)


def sort_pairs(n):
    pairs, p = [], 1
    while p < n:
        k = p
        while k >= 1:
            for j in range(k % p, n - k, 2 * k):
                for i in range(min(k, n - j - k)):
                    if (i + j) // (2 * p) == (i + j + k) // (2 * p):
                        pairs.append((i + j, i + j + k))
            k //= 2
        p *= 2
    return pairs


def sort_down(values):
    values = list(values)
    for i, j in sort_pairs(len(values)):
        values[i], values[j] = jnp.maximum(values[i], values[j]), jnp.minimum(values[i], values[j])
    return values


def merge_down(left, right, keep=TOPK):
    left = list(left) + [False] * (keep - len(left))
    right = list(right) + [False] * (keep - len(right))

    def order(u, v):
        if u is None or v is False:
            return u, v
        if v is None or u is False:
            return v, u
        return jnp.maximum(u, v), jnp.minimum(u, v)

    line = [order(left[i], right[keep - 1 - i])[0] for i in range(keep)] + [None] * (32 - keep)
    gap = 16
    while gap:
        for i in range(32):
            if not i & gap:
                line[i], line[i + gap] = order(line[i], line[i + gap])
        gap //= 2
    return line[32 - keep :]


def head_kernel(x_ref, ids_ref, own_ref, other_ref, st_ref, LT, M, Q, V, *, columns):
    step = pl.program_id(0)
    rows, width = x_ref.shape[0] * x_ref.shape[1], x_ref.shape[2]
    wide = own_ref.shape[0]
    half = pl.num_programs(0) // 2

    def logits_of(w_ref):
        x = x_ref[...].reshape(rows, width)
        logits = lax.dot_general(
            w_ref[...], x, (((1,), (1,)), ((), ())), preferred_element_type=jnp.float32
        )
        place = lax.broadcasted_iota(jnp.int32, (wide, rows), 0) + lax.rem(step, half) * wide
        LT[pl.ds(pl.multiple_of(step * wide, wide), wide), :] = jnp.where(place < columns, logits, NEG)

    @pl.when(step < half)
    def _():
        logits_of(own_ref)

    @pl.when(step >= half)
    def _():
        logits_of(other_ref)

    @pl.when(step == pl.num_programs(0) - 1)
    def _():
        levels, lane_tiles = 16, rows // 128
        deep = LT.shape[0] // levels
        place = lax.axis_index(CORE), [lax.axis_index(n) for n in AXES]
        chip = (place[1][0] * N + place[1][1]) * N + place[1][2]
        first = (place[0] * N**3 + chip) * columns
        second = ((1 - place[0]) * N**3 + chip) * columns
        for t in range(lane_tiles):
            lanes = pl.ds(128 * t, 128)
            ids = ids_ref[:, lanes]

            @pl.loop(0, deep // 16)
            def _(j):
                both = []
                for side in range(2):
                    at = pl.multiple_of(side * (deep // 2) + j * 8, 8)
                    both.append(sort_down([LT[pl.ds(l * deep + at, 8), lanes] for l in range(levels)]))
                for l, value in enumerate(merge_down(*both)):
                    M[l, pl.ds(pl.multiple_of(j * 8, 8), 8), lanes] = value

            have = deep // 16
            while have > 1:
                have //= 2

                @pl.loop(0, have)
                def _(j):
                    both = []
                    for side in range(2):
                        at = pl.multiple_of((side * have + j) * 8, 8)
                        both.append([M[l, pl.ds(at, 8), lanes] for l in range(TOPK)])
                    for l, value in enumerate(merge_down(*both)):
                        M[l, pl.ds(pl.multiple_of(j * 8, 8), 8), lanes] = value

            top = [M[l, pl.ds(0, 8), lanes] for l in range(TOPK)]
            for shift in (4, 2, 1):
                top = merge_down(top, [pltpu.roll(v, shift, 0) for v in top])
            peak = top[0]

            def body(j, carry):
                total, hit = carry
                at = pl.multiple_of(j * 8, 8)
                value = LT[pl.ds(at, 8), lanes]
                row = lax.broadcasted_iota(jnp.int32, (8, 128), 0) + at
                late = row >= LT.shape[0] // 2
                column = jnp.where(late, row - LT.shape[0] // 2, row)
                token = column + jnp.where(late, second, first)
                same = (token == ids) & (column < columns)
                return total + jnp.exp(value - peak), hit + jnp.where(same, value, 0.0)

            zero = jnp.zeros((8, 128), jnp.float32)
            total, hit = lax.fori_loop(0, LT.shape[0] // 8, body, (zero, zero), unroll=8)
            for l in range(TOPK):
                Q[pl.ds(l, 1), lanes] = top[l][0:1]
            Q[pl.ds(TOPK, 1), lanes] = jnp.sum(total, axis=0, keepdims=True)
            Q[pl.ds(TOPK + 1, 1), lanes] = jnp.sum(hit, axis=0, keepdims=True)
            Q[pl.ds(TOPK + 2, 2), lanes] = jnp.zeros((2, 128), jnp.float32)
            Q[pl.ds(24, 104), lanes] = jnp.zeros((104, 128), jnp.float32)
        V[...] = Q[...].T
        for i in range(N):
            for j in range(N):
                for k in range(N):
                    st_ref[i, j, k] = V[pl.ds(((i * N + j) * N + k) * 4, 4), :]


def head_stats(x, ids, own, other):
    columns, width = own.shape
    wide = 256
    half = -(-columns // wide)
    rows = x.shape[0] * x.shape[1]
    f32 = jnp.float32
    return pl.pallas_call(
        functools.partial(head_kernel, columns=columns),
        out_shape=jax.ShapeDtypeStruct((N, N, N, 4, 128), f32),
        grid=(2 * half,),
        in_specs=[
            pl.BlockSpec(x.shape, lambda s: (0, 0, 0), pipeline_mode=pl.Buffered(1)),
            pl.BlockSpec(ids.shape, lambda s: (0, 0)),
            pl.BlockSpec((wide, width), lambda s: (jnp.minimum(s, half - 1), 0)),
            pl.BlockSpec((wide, width), lambda s: (jnp.maximum(s - half, 0), 0)),
        ],
        out_specs=pl.BlockSpec((N, N, N, 4, 128), lambda s: (0, 0, 0, 0, 0)),
        scratch_shapes=[
            pltpu.VMEM((2 * half * wide, rows), f32),
            pltpu.VMEM((TOPK, half * wide // 16, rows), f32),
            pltpu.VMEM((128, rows), f32),
            pltpu.VMEM((rows, 128), f32),
        ],
        compiler_params=pltpu.CompilerParams(dimension_semantics=("arbitrary",), vmem_limit_bytes=60 << 20),
        name="head_stats",
    )(x, ids, own, other)


def finish_kernel(st_ref, sid_ref, lp_ref, ln_ref, tm_ref, sq_ref, U1, U2, U3, B, Q, A, a_s, a_r, q_s, q_r):
    meet()
    mail = Mail(a_s, a_r)
    for k in (1, 3, 2):
        mail.send(1, st_ref.at[:, :, k], U1.at[N - k], toward(2, k))
    U1[0] = st_ref[:, :, 0]
    mail.received(1)
    for k in (1, 3, 2):
        mail.send(2, U1.at[:, :, k], U2.at[N - k], toward(1, k))
    U2[0] = U1[:, :, 0]
    mail.received(2)
    for k in (1, 3, 2):
        mail.send(3, U2.at[:, :, k], U3.at[N - k], toward(0, k))
    U3[0] = U2[:, :, 0]
    mail.received(3)
    for i in range(N):
        for j in range(N):
            for k in range(N):
                B[pl.ds(((i * N + j) * N + k) * 4, 4), :] = U3[i, j, k]
    Q[...] = B[...].T

    def line(l):
        return [Q[pl.ds(l, 1), pl.ds(128 * t, 128)] for t in range(2)]

    lists = [line(l) for l in range(TOPK)]
    top = merge_down([v[0] for v in lists], [v[1] for v in lists])
    for shift in (64, 32, 16, 8, 4):
        top = merge_down(top, [pltpu.roll(v, shift, 1) for v in top])
    peak = top[0]
    sums, hits = line(TOPK), line(TOPK + 1)
    total = sum(s * jnp.exp(v - peak) for s, v in zip(sums, lists[0]))
    hit = hits[0] + hits[1]
    for shift in (64, 32, 16, 8, 4):
        total = total + pltpu.roll(total, shift, 1)
        hit = hit + pltpu.roll(hit, shift, 1)
    log_norm = peak + jnp.log(total)
    mass = sum(jnp.exp(v - log_norm) for v in top)
    logprob = hit - log_norm
    for ref, value in ((lp_ref, logprob), (ln_ref, log_norm), (tm_ref, mass)):
        ref[0:1, :] = value[:, 0:2]
        ref[1:2, :] = pltpu.roll(value, 126, 1)[:, 0:2]

    lane = lax.broadcasted_iota(jnp.int32, (1, 128), 1)
    turned = [logprob] + [pltpu.roll(logprob, j, 1) for j in (1, 2, 3)]
    part = jnp.zeros((1, 128), jnp.float32)
    for t in range(4):
        spread = turned[0]
        for j in (1, 2, 3):
            spread = jnp.where(lax.rem(lane - t + 4, 4) == j, turned[j], spread)
        mine = (lane // SEQS == t // 2) & (lax.rem(lane, SEQS) == sid_ref[t // 2, t % 2])
        part = part + jnp.where(mine, spread, 0.0)
    A[0, 0] = jnp.broadcast_to(part, (8, 128))
    seq = Mail(q_s, q_r)
    seq.send(0, A.at[0, 0], A.at[0, 1], partner())
    seq.received(0)
    both = A[0, 0] + A[0, 1]
    for axis in range(3):
        A[axis + 1, 0] = both
        for k in (1, 3, 2):
            seq.send(axis + 1, A.at[axis + 1, 0], A.at[axis + 1, N - k], toward(axis, k))
        seq.received(axis + 1)
        got = [A[axis + 1, k] for k in range(N)]
        both = (got[0] + got[2]) + (got[1] + got[3])
    sq_ref[0:1, :] = both[0:1, 0:SEQS]
    sq_ref[1:2, :] = pltpu.roll(both, 128 - SEQS, 1)[0:1, 0:SEQS]
    mail.all_sent()
    seq.all_sent()


def finish(stats, seq_ids):
    f32 = jnp.float32
    vmem = pl.BlockSpec(memory_space=pltpu.VMEM)
    dma = lambda n: pltpu.SemaphoreType.DMA((n,))
    small = jax.ShapeDtypeStruct(seq_ids.shape, f32)
    tile = (4, 128)
    return pl.pallas_call(
        finish_kernel,
        out_shape=(small, small, small, jax.ShapeDtypeStruct((2, SEQS), f32)),
        in_specs=[vmem, pl.BlockSpec(memory_space=pltpu.SMEM)],
        out_specs=(vmem, vmem, vmem, vmem),
        scratch_shapes=[
            pltpu.VMEM((N, N, N) + tile, f32),
            pltpu.VMEM((N, N, N) + tile, f32),
            pltpu.VMEM((N, N, N) + tile, f32),
            pltpu.VMEM((N**3 * 4, 128), f32),
            pltpu.VMEM((128, N**3 * 4), f32),
            pltpu.VMEM((4, N, 8, 128), f32),
            dma(9), dma(9), dma(10), dma(10),
        ],
        compiler_params=pltpu.CompilerParams(collective_id=1, has_side_effects=True),
        name="finish",
    )(stats, seq_ids)


def body(hidden_in, gain_ffn, w_gate, w_up, w_down, gain_final, head_weight, sampled_ids, seq_ids):
    batches, own, width = hidden_in.shape
    place = jnp.arange(N**3 * 4, dtype=jnp.int32)
    chip = jnp.int32(0)
    for n, name in enumerate(AXES):
        offset = place // (4 * N ** (2 - n)) % N
        chip = chip * N + (lax.axis_index(name) + offset) % N
    device = lax.axis_index(CORE) * N**3 + chip
    slot = (place % 4) // own * sampled_ids.shape[1] + device * own + place % own
    flat = sampled_ids.reshape(-1)
    ids = jnp.sum(jnp.where(slot[None, :] == jnp.arange(flat.size)[:, None], flat[:, None], 0), axis=0)

    head = head_weight.T
    x, other_head = dense_block(
        hidden_in.reshape(batches * own, width), gain_ffn.reshape(1, width), gain_final.reshape(1, width),
        w_gate.T, w_up.T, w_down, head,
    )
    stats = head_stats(x, ids.reshape(1, -1), head, other_head)
    return tuple(finish(stats, seq_ids))


def solution(mesh):
    split = Mesh(mesh.devices.reshape(mesh.shape["section"], N, N, N), EVERY)
    rows = P(None, EVERY)
    return jax.shard_map(
        body,
        mesh=split,
        in_specs=(P(None, EVERY, None), P(), rows, rows, P(EVERY, None), P(), rows, P(), rows),
        out_specs=(rows, rows, rows, P()),
        check_vma=False,
    )
```

```python
import functools

import jax
import jax.numpy as jnp
from jax import lax
from jax.experimental import pallas as pl
from jax.experimental.pallas import tpu as pltpu
from jax.sharding import Mesh
from jax.sharding import PartitionSpec as P

SEQS = 8
TOPK = 20
EPS = 1e-06
NEG = -3.0e38
MESH = pl.DeviceIdType.MESH
CORE = "section"
AXES = ("x", "z", "y")
EVERY = (CORE,) + AXES
ORDERS = ((0, 1, 2), (1, 2, 0), (2, 0, 1))
N = 4


def pick(sel):
    return tuple(sel.get(i, slice(None)) for i in range(3))


def column_groups(width):
    tiles = width // 128
    cuts = [0, (tiles + 2) // 3, (2 * tiles + 2) // 3, tiles]
    waves = [[], []]
    for q in range(3):
        size = cuts[q + 1] - cuts[q]
        half = (size + 1) // 2 if q < 2 else size // 2 - (size // 2) % 2
        at = 128 * cuts[q]
        waves[0].append((at, 128 * half))
        waves[1].append((at + 128 * half, 128 * (size - half)))
    return waves


def toward(axis, k):
    name = AXES[axis]
    return {name: lax.rem(lax.axis_index(name) + k, N)}


def partner():
    return {CORE: 1 - lax.axis_index(CORE)}


def greet():
    barrier = pltpu.get_barrier_semaphore()
    for axis in range(3):
        for k in (1, 2, 3):
            pl.semaphore_signal(barrier, inc=1, device_id=toward(axis, k), device_id_type=MESH)
    pl.semaphore_signal(barrier, inc=1, device_id=partner(), device_id_type=MESH)


def met():
    pl.semaphore_wait(pltpu.get_barrier_semaphore(), 10)


class Mail:
    def __init__(self, send_sem, recv_sem):
        self.send_sem, self.recv_sem = send_sem, recv_sem
        self.copies, self.count = {}, 0

    def send(self, tag, src, dst, device):
        copy = pltpu.make_async_remote_copy(
            src_ref=src,
            dst_ref=dst,
            send_sem=self.send_sem.at[self.count],
            recv_sem=self.recv_sem.at[self.count],
            device_id=device,
            device_id_type=MESH,
        )
        copy.start()
        self.count += 1
        self.copies.setdefault(tag, []).append(copy)

    def received(self, tag):
        for copy in self.copies[tag]:
            copy.wait_recv()

    def all_sent(self):
        for copies in self.copies.values():
            for copy in copies:
                copy.wait_send()


WAVES = (0, 1)


def gather_start(buf, mail, groups):
    def go(s, q, tag, sel, axis):
        for k in (1, 3, 2):
            src, dst = dict(sel), dict(sel)
            src[axis], dst[axis] = 0, N - k
            rest = (slice(None), pl.ds(*groups[s][q]))
            mail.send((s, q, tag), buf.at[pick(src) + rest], buf.at[pick(dst) + rest], toward(axis, k))

    others = pl.ds(1, 3)
    every = [(s, q) + ORDERS[q] for s in WAVES for q in range(3)]
    for s, q, a, b, c in every:
        go(s, q, "a", {b: 0, c: 0}, a)
    for s, q, a, b, c in every:
        go(s, q, "b0", {a: 0, c: 0}, b)
    for s, q, a, b, c in every:
        go(s, q, "c0", {a: 0, b: 0}, c)
    for s, q, a, b, c in every:
        mail.received((s, q, "a"))
        go(s, q, "b1", {a: others, c: 0}, b)
    for s, q, a, b, c in every:
        go(s, q, "c1", {a: others, b: 0}, c)
    for s, q, a, b, c in every:
        mail.received((s, q, "b0"))
        go(s, q, "c2", {a: 0, b: others}, c)
    for s, q, a, b, c in every:
        mail.received((s, q, "b1"))
        go(s, q, "c3", {a: others, b: others}, c)


def gather_end(buf, out, mail, groups, s):
    for tag in ("c0", "c1", "c2", "c3"):
        for q in range(3):
            mail.received((s, q, tag))

    @pl.loop(0, N)
    def _(i):
        @pl.loop(0, N)
        def _(j):
            for k in range(N):
                for q in range(3):
                    cols = pl.ds(*groups[s][q])
                    out[i * N + j, pl.ds(4 * k, 4), cols] = buf[i, j, k, :, cols]


def rms(wide, gain):
    mean = jnp.mean(wide * wide, axis=-1, keepdims=True)
    return (wide * lax.rsqrt(mean + EPS) * gain).astype(jnp.bfloat16)


def by_tokens(weight, x, groups, s):
    rows = x.shape[0] * x.shape[1]
    total = None
    for q in range(3):
        cols = pl.ds(*groups[s][q])
        part = lax.dot_general(
            weight(cols), x[:, :, cols].reshape(rows, groups[s][q][1]), (((1,), (1,)), ((), ())),
            preferred_element_type=jnp.float32,
        )
        total = part if total is None else total + part
    return total


def order_ids(ids_ref, IDS, Q, V, own):
    Q[...] = jnp.zeros_like(Q)
    Q[0:2, :] = ids_ref[...].astype(jnp.float32)
    V[...] = Q[...].T
    size = ids_ref.shape[1]
    place = lax.broadcasted_iota(jnp.int32, (size, N**3 * 4), 1)
    row = lax.broadcasted_iota(jnp.int32, (size, N**3 * 4), 0)
    chip = jnp.zeros_like(place)
    for n, name in enumerate(AXES):
        chip = chip * N + lax.rem(lax.axis_index(name) + lax.rem(place // (4 * N ** (2 - n)), N), N)
    slot = (lax.axis_index(CORE) * N**3 + chip) * own + lax.rem(place, own)
    value = jnp.where(lax.rem(place, 4) // own == 0, V[:, 0:1], V[:, 1:2])
    IDS[...] = jnp.sum(jnp.where(row == slot, value, 0.0), axis=0, keepdims=True).astype(jnp.int32)


def sort_pairs(n):
    pairs, p = [], 1
    while p < n:
        k = p
        while k >= 1:
            for j in range(k % p, n - k, 2 * k):
                for i in range(min(k, n - j - k)):
                    if (i + j) // (2 * p) == (i + j + k) // (2 * p):
                        pairs.append((i + j, i + j + k))
            k //= 2
        p *= 2
    return pairs


def sort_down(values):
    values = list(values)
    for i, j in sort_pairs(len(values)):
        values[i], values[j] = jnp.maximum(values[i], values[j]), jnp.minimum(values[i], values[j])
    return values


def merge_down(left, right, keep=TOPK):
    left = list(left) + [False] * (keep - len(left))
    right = list(right) + [False] * (keep - len(right))

    def order(u, v):
        if u is None or v is False:
            return u, v
        if v is None or u is False:
            return v, u
        return jnp.maximum(u, v), jnp.minimum(u, v)

    line = [order(left[i], right[keep - 1 - i])[0] for i in range(keep)] + [None] * (32 - keep)
    gap = 16
    while gap:
        for i in range(32):
            if not i & gap:
                line[i], line[i + gap] = order(line[i], line[i + gap])
        gap //= 2
    return line[32 - keep :]


def slot_stats(LT, M, Q, V, IDS, ST, columns):
    levels, rows = 16, LT.shape[1]
    deep = LT.shape[0] // levels
    chip = (lax.axis_index("x") * N + lax.axis_index("z")) * N + lax.axis_index("y")
    core = lax.axis_index(CORE)
    first = (core * N**3 + chip) * columns
    second = ((1 - core) * N**3 + chip) * columns
    for t in range(rows // 128):
        lanes = pl.ds(128 * t, 128)
        ids = IDS[:, lanes]

        @pl.loop(0, deep // 16)
        def _(j):
            both = []
            for side in range(2):
                at = pl.multiple_of(side * (deep // 2) + j * 8, 8)
                both.append(sort_down([LT[pl.ds(l * deep + at, 8), lanes] for l in range(levels)]))
            for l, value in enumerate(merge_down(*both)):
                M[l, pl.ds(pl.multiple_of(j * 8, 8), 8), lanes] = value

        have = deep // 16
        while have > 1:
            have //= 2

            @pl.loop(0, have)
            def _(j):
                both = []
                for side in range(2):
                    at = pl.multiple_of((side * have + j) * 8, 8)
                    both.append([M[l, pl.ds(at, 8), lanes] for l in range(TOPK)])
                for l, value in enumerate(merge_down(*both)):
                    M[l, pl.ds(pl.multiple_of(j * 8, 8), 8), lanes] = value

        top = [M[l, pl.ds(0, 8), lanes] for l in range(TOPK)]
        for shift in (4, 2, 1):
            top = merge_down(top, [pltpu.roll(v, shift, 0) for v in top])
        peak = top[0]

        def body(j, carry):
            total, hit = carry
            at = pl.multiple_of(j * 8, 8)
            value = LT[pl.ds(at, 8), lanes]
            row = lax.broadcasted_iota(jnp.int32, (8, 128), 0) + at
            late = row >= LT.shape[0] // 2
            column = jnp.where(late, row - LT.shape[0] // 2, row)
            token = column + jnp.where(late, second, first)
            same = (token == ids) & (column < columns)
            return total + jnp.exp(value - peak), hit + jnp.where(same, value, 0.0)

        zero = jnp.zeros((8, 128), jnp.float32)
        total, hit = lax.fori_loop(0, LT.shape[0] // 8, body, (zero, zero), unroll=8)
        for l in range(TOPK):
            Q[pl.ds(l, 1), lanes] = top[l][0:1]
        Q[pl.ds(TOPK, 1), lanes] = jnp.sum(total, axis=0, keepdims=True)
        Q[pl.ds(TOPK + 1, 1), lanes] = jnp.sum(hit, axis=0, keepdims=True)
    V[...] = Q[...].T
    for i in range(N):
        for j in range(N):
            for k in range(N):
                ST[i, j, k] = V[pl.ds(((i * N + j) * N + k) * 4, 4), :]


def merged(U3, V, Q):
    for i in range(N):
        for j in range(N):
            for k in range(N):
                V[pl.ds(((i * N + j) * N + k) * 4, 4), :] = U3[i, j, k]
    Q[...] = V[...].T

    def line(l):
        return [Q[pl.ds(l, 1), pl.ds(128 * t, 128)] for t in range(2)]

    lists = [line(l) for l in range(TOPK)]
    top = merge_down([v[0] for v in lists], [v[1] for v in lists])
    for shift in (64, 32, 16, 8, 4):
        top = merge_down(top, [pltpu.roll(v, shift, 1) for v in top])
    peak = top[0]
    sums, hits = line(TOPK), line(TOPK + 1)
    total = sum(s * jnp.exp(v - peak) for s, v in zip(sums, lists[0]))
    hit = hits[0] + hits[1]
    for shift in (64, 32, 16, 8, 4):
        total = total + pltpu.roll(total, shift, 1)
        hit = hit + pltpu.roll(hit, shift, 1)
    log_norm = peak + jnp.log(total)
    mass = sum(jnp.exp(v - log_norm) for v in top)
    return hit - log_norm, log_norm, mass


def by_sequence(logprob, sid_ref):
    lane = lax.broadcasted_iota(jnp.int32, (1, 128), 1)
    turned = [logprob] + [pltpu.roll(logprob, j, 1) for j in (1, 2, 3)]
    part = jnp.zeros((1, 128), jnp.float32)
    for t in range(4):
        spread = turned[0]
        for j in (1, 2, 3):
            spread = jnp.where(lax.rem(lane - t + 4, 4) == j, turned[j], spread)
        mine = (lane // SEQS == t // 2) & (lax.rem(lane, SEQS) == sid_ref[t // 2, t % 2])
        part = part + jnp.where(mine, spread, 0.0)
    return jnp.broadcast_to(part, (8, 128))


def score_kernel(
    h_ref, gf_ref, gl_ref, wg_ref, wu_ref, wd_ref, hw_ref, ids_ref, sid_ref,
    out_ref,
    HS, G, X, S, R1, R2, R3, T1, T2, F, PB, W, WD, Y, ACT, HB, LT, M, Q, V, IDS, ST, U1, U2, U3, A,
    own_s, swap_s, swap_r, g_s, g_r, r_s, r_r, g2_s, g2_r, a_s, a_r, q_s, q_r,
):
    width = h_ref.shape[-1]
    groups = column_groups(width)
    rows = N**3 * 4
    hidden = W.shape[1]
    columns = HB.shape[1]
    loads = []
    for n, (src, dst) in enumerate(((wg_ref, W.at[0]), (wu_ref, W.at[1]), (wd_ref, WD.at[0]))):
        copy = pltpu.make_async_copy(src, dst, own_s.at[n])
        copy.start()
        loads.append(copy)
    greet()
    own = h_ref.shape[1]
    for m in range(h_ref.shape[0]):
        HS[pl.ds(m * own, own), :] = h_ref[m].astype(jnp.float32)
    G[0, 0, 0] = rms(HS[...], gf_ref[...])
    met()
    mail = Mail(g_s, g_r)
    swap = Mail(swap_s, swap_r)
    for tag, src, dst in (("g", wg_ref, W.at[2]), ("u", wu_ref, W.at[3]), ("d", wd_ref, WD.at[1])):
        swap.send(tag, src, dst, partner())
    gather_start(G, mail, groups)
    order_ids(ids_ref, IDS, Q, V, own)
    for copy in loads[:2]:
        copy.wait()
    for tag in ("g", "u"):
        swap.received(tag)
    for s in WAVES:
        gather_end(G, X, mail, groups, s)
        part = by_tokens(lambda cols: W[:, :, cols].reshape(4 * hidden, cols.size), X, groups, s)
        Y[...] = part if s == 0 else Y[...] + part
    loads[2].wait()
    swap.received("d")
    swap.send("h", hw_ref, HB.at[1], partner())
    own_head = pltpu.make_async_copy(hw_ref, HB.at[0], own_s.at[3])
    own_head.start()
    acts = []
    for p in range(2):
        gate, up = Y[pl.ds(2 * p * hidden, hidden), :], Y[pl.ds((2 * p + 1) * hidden, hidden), :]
        acts.append(gate / (1.0 + jnp.exp(-gate)) * up)
    ACT[...] = jnp.concatenate(acts, axis=0).T.astype(jnp.bfloat16)
    mail.all_sent()

    red = Mail(r_s, r_r)
    wide = PB.shape[-1]

    def down(at, size):
        cols = pl.ds(at, size)
        part = jnp.dot(ACT[...], WD[:, :, cols].reshape(2 * hidden, size), preferred_element_type=jnp.float32)
        PB[:, :, pl.ds(0, size)] = part.astype(jnp.bfloat16).reshape(N * N, N * 4, size)
        for i in range(N):
            for j in range(N):
                for k in range(N):
                    S[i, j, k, :, cols] = PB[i * N + j, pl.ds(4 * k, 4), pl.ds(0, size)]

    every = [(s, q, pl.ds(*groups[s][q])) + ORDERS[q] for s in WAVES for q in range(3)]
    for s, q, cols, a, b, c in every:
        start, size = groups[s][q]

        @pl.loop(0, size // wide)
        def _(n):
            down(pl.multiple_of(start + n * wide, 128), wide)

        if size % wide:
            down(start + size // wide * wide, size % wide)
        rest = (slice(None), cols)
        for k in (2, 1, 3):
            red.send((s, q, 1), S.at[pick({c: k}) + rest], R1.at[(k - 1, slice(None), slice(None)) + rest], toward(c, k))
    for s, q, cols, a, b, c in every:
        red.received((s, q, 1))

        @pl.loop(0, N)
        def _(i):
            @pl.loop(0, N)
            def _(j):
                left = [i, j]
                sel = {ax: left.pop(0) for ax in range(3) if ax != c}
                sel[c] = 0
                total = S[pick(sel) + (slice(None), cols)].astype(jnp.float32)
                for k in range(3):
                    total += R1[k, i, j, :, cols].astype(jnp.float32)
                T1[i, j, :, cols] = total.astype(jnp.bfloat16)

        first = min(a, b)
        for k in (2, 1, 3):
            src = T1.at[k, :, :, cols] if b == first else T1.at[:, k, :, cols]
            red.send((s, q, 2), src, R2.at[k - 1, :, :, cols], toward(b, k))
    for s, q, cols, a, b, c in every:
        red.received((s, q, 2))
        first = min(a, b)
        for i in range(N):
            total = (T1[0, i, :, cols] if b == first else T1[i, 0, :, cols]).astype(jnp.float32)
            for k in range(3):
                total += R2[k, i, :, cols].astype(jnp.float32)
            T2[i, :, cols] = total.astype(jnp.bfloat16)
        for k in (2, 1, 3):
            red.send((s, q, 3), T2.at[k, :, cols], R3.at[k - 1, :, cols], toward(a, k))
    for s, q, cols, a, b, c in every:
        red.received((s, q, 3))
        total = T2[0, :, cols].astype(jnp.float32)
        for k in range(3):
            total += R3[k, :, cols].astype(jnp.float32)
        F[:, cols] = total

    residual = (HS[...] + F[...]).astype(jnp.bfloat16)
    G[0, 0, 0] = rms(residual.astype(jnp.float32), gl_ref[...])
    mail2 = Mail(g2_s, g2_r)
    gather_start(G, mail2, groups)
    swap.received("h")
    own_head.wait()
    half, tall = LT.shape[0] // 2, 256
    for s in WAVES:
        gather_end(G, X, mail2, groups, s)
        for p in range(2):
            if s == 0:
                LT[pl.ds(p * half + columns // 8 * 8, half - columns // 8 * 8), :] = jnp.full(
                    (half - columns // 8 * 8, rows), NEG, jnp.float32
                )

            def logits(at, size):
                part = by_tokens(lambda cols: HB[p, pl.ds(at, size), cols], X, groups, s)
                to = pl.ds(p * half + at, size)
                LT[to, :] = part if s == 0 else LT[to, :] + part

            @pl.loop(0, columns // tall)
            def _(n):
                logits(pl.multiple_of(n * tall, tall), tall)

            if columns % tall:
                logits(columns // tall * tall, columns % tall)

    slot_stats(LT, M, Q, V, IDS, ST, columns)

    stats = Mail(a_s, a_r)
    for k in (2, 1, 3):
        stats.send(1, ST.at[:, :, k], U1.at[N - k], toward(2, k))
    U1[0] = ST[:, :, 0]
    stats.received(1)
    for k in (2, 1, 3):
        stats.send(2, U1.at[:, :, k], U2.at[N - k], toward(1, k))
    U2[0] = U1[:, :, 0]
    stats.received(2)
    for k in (2, 1, 3):
        stats.send(3, U2.at[:, :, k], U3.at[N - k], toward(0, k))
    U3[0] = U2[:, :, 0]
    stats.received(3)
    logprob, log_norm, mass = merged(U3, V, Q)

    A[0, 0] = by_sequence(logprob, sid_ref)
    seq = Mail(q_s, q_r)
    seq.send(0, A.at[0, 0], A.at[0, 1], partner())
    seq.received(0)
    both = A[0, 0] + A[0, 1]
    for axis in range(3):
        A[axis + 1, 0] = both
        for k in (2, 1, 3):
            seq.send(axis + 1, A.at[axis + 1, 0], A.at[axis + 1, N - k], toward(axis, k))
        seq.received(axis + 1)
        got = [A[axis + 1, k] for k in range(N)]
        both = (got[0] + got[2]) + (got[1] + got[3])
    for n, value in enumerate((logprob, log_norm, mass, both[0:1])):
        out_ref[pl.ds(n, 1), :] = value
    out_ref[4:8, :] = jnp.zeros((4, 128), jnp.float32)
    for m in (swap, red, mail2, stats, seq):
        m.all_sent()


def score(h, gain_ffn, gain_final, w_gate, w_up, w_down, head, ids, seq_ids):
    hidden, width = w_gate.shape
    columns = head.shape[0]
    half = -(-columns // 256) * 256
    rows = N**3 * 4
    bf16, f32 = jnp.bfloat16, jnp.float32
    vmem, anywhere = pl.BlockSpec(memory_space=pltpu.VMEM), pl.BlockSpec(memory_space=pl.ANY)
    dma = lambda n: pltpu.SemaphoreType.DMA((n,))
    stat = pltpu.VMEM((N, N, N, 4, 128), f32)
    return pl.pallas_call(
        score_kernel,
        out_shape=jax.ShapeDtypeStruct((8, 128), f32),
        in_specs=[vmem, vmem, vmem, anywhere, anywhere, anywhere, anywhere, vmem, pl.BlockSpec(memory_space=pltpu.SMEM)],
        out_specs=vmem,
        scratch_shapes=[
            pltpu.VMEM((4, width), f32),
            pltpu.VMEM((N, N, N, 4, width), bf16),
            pltpu.VMEM((N * N, N * 4, width), bf16),
            pltpu.VMEM((N, N, N, 4, width), bf16),
            pltpu.VMEM((3, N, N, 4, width), bf16),
            pltpu.VMEM((3, N, 4, width), bf16),
            pltpu.VMEM((3, 4, width), bf16),
            pltpu.VMEM((N, N, 4, width), bf16),
            pltpu.VMEM((N, 4, width), bf16),
            pltpu.VMEM((4, width), f32),
            pltpu.VMEM((N * N, N * 4, 256), bf16),
            pltpu.VMEM((4, hidden, width), bf16),
            pltpu.VMEM((2, hidden, width), bf16),
            pltpu.VMEM((4 * hidden, rows), f32),
            pltpu.VMEM((rows, 2 * hidden), bf16),
            pltpu.VMEM((2, columns, width), bf16),
            pltpu.VMEM((2 * half, rows), f32),
            pltpu.VMEM((TOPK, half // 16, rows), f32),
            pltpu.VMEM((128, rows), f32),
            pltpu.VMEM((rows, 128), f32),
            pltpu.VMEM((1, rows), jnp.int32),
            stat, stat, stat, stat,
            pltpu.VMEM((4, N, 8, 128), f32),
            dma(4), dma(4), dma(4), dma(126), dma(126), dma(54), dma(54), dma(126), dma(126), dma(9), dma(9), dma(10), dma(10),
        ],
        compiler_params=pltpu.CompilerParams(collective_id=0, has_side_effects=True, vmem_limit_bytes=67043328),
        name="score",
    )(h, gain_ffn, gain_final, w_gate, w_up, w_down, head, ids, seq_ids)


def emit_kernel(x_ref, lp_ref, ln_ref, tm_ref, sq_ref):
    for n, ref in enumerate((lp_ref, ln_ref, tm_ref, sq_ref)):
        size = ref.shape[1]
        line = x_ref[pl.ds(n, 1), :]
        ref[0:1, :] = line[:, 0:size]
        ref[1:2, :] = pltpu.roll(line, 128 - size, 1)[:, 0:size]


def emit(x, own):
    f32 = jnp.float32
    small = jax.ShapeDtypeStruct((2, own), f32)
    return pl.pallas_call(
        emit_kernel, out_shape=(small, small, small, jax.ShapeDtypeStruct((2, SEQS), f32)), name="emit"
    )(x)


def body(hidden_in, gain_ffn, w_gate, w_up, w_down, gain_final, head_weight, sampled_ids, seq_ids):
    width = hidden_in.shape[-1]
    packed = score(
        hidden_in, gain_ffn.reshape(1, width), gain_final.reshape(1, width),
        w_gate.T, w_up.T, w_down, head_weight.T, sampled_ids, seq_ids,
    )
    return tuple(emit(packed, hidden_in.shape[1]))


def solution(mesh):
    split = Mesh(mesh.devices.reshape(mesh.shape["section"], N, N, N), EVERY)
    rows = P(None, EVERY)
    return jax.shard_map(
        body,
        mesh=split,
        in_specs=(P(None, EVERY, None), P(), rows, rows, P(EVERY, None), P(), rows, P(), rows),
        out_specs=(rows, rows, rows, P()),
        check_vma=False,
    )
```

```python
import functools

import jax
import jax.numpy as jnp
from jax import lax
from jax.experimental import pallas as pl
from jax.experimental.pallas import tpu as pltpu
from jax.sharding import Mesh
from jax.sharding import PartitionSpec as P

SEQS = 8
TOPK = 20
EPS = 1e-06
NEG = -3.0e38
MESH = pl.DeviceIdType.MESH
CORE = "section"
AXES = ("x", "z", "y")
EVERY = (CORE,) + AXES
ORDERS = ((0, 1, 2), (1, 2, 0), (2, 0, 1))
N = 4


def pick(sel):
    return tuple(sel.get(i, slice(None)) for i in range(3))


def column_groups(width):
    tiles = width // 128
    cuts = [0, (tiles + 2) // 3, (2 * tiles + 2) // 3, tiles]
    waves = [[], []]
    for q in range(3):
        size = cuts[q + 1] - cuts[q]
        half = (size + 1) // 2 if q < 2 else size // 2 - (size // 2) % 2
        at = 128 * cuts[q]
        waves[0].append((at, 128 * half))
        waves[1].append((at + 128 * half, 128 * (size - half)))
    return waves


def toward(axis, k):
    name = AXES[axis]
    return {name: lax.rem(lax.axis_index(name) + k, N)}


def partner():
    return {CORE: 1 - lax.axis_index(CORE)}


def greet():
    barrier = pltpu.get_barrier_semaphore()
    for axis in range(3):
        for k in (1, 2, 3):
            pl.semaphore_signal(barrier, inc=1, device_id=toward(axis, k), device_id_type=MESH)
    pl.semaphore_signal(barrier, inc=1, device_id=partner(), device_id_type=MESH)


def met():
    pl.semaphore_wait(pltpu.get_barrier_semaphore(), 10)


class Mail:
    def __init__(self, send_sem, recv_sem):
        self.send_sem, self.recv_sem = send_sem, recv_sem
        self.copies, self.count = {}, 0

    def send(self, tag, src, dst, device):
        copy = pltpu.make_async_remote_copy(
            src_ref=src,
            dst_ref=dst,
            send_sem=self.send_sem.at[self.count],
            recv_sem=self.recv_sem.at[self.count],
            device_id=device,
            device_id_type=MESH,
        )
        copy.start()
        self.count += 1
        self.copies.setdefault(tag, []).append(copy)

    def received(self, tag):
        for copy in self.copies[tag]:
            copy.wait_recv()

    def all_sent(self):
        for copies in self.copies.values():
            for copy in copies:
                copy.wait_send()


WAVES = (0, 1)


def gather_start(buf, mail, groups):
    def go(s, q, tag, sel, axis):
        for k in (1, 3, 2):
            src, dst = dict(sel), dict(sel)
            src[axis], dst[axis] = 0, N - k
            rest = (slice(None), pl.ds(*groups[s][q]))
            mail.send((s, q, tag), buf.at[pick(src) + rest], buf.at[pick(dst) + rest], toward(axis, k))

    others = pl.ds(1, 3)
    def each(s, tag, sel, along, after=None):
        for q, axes in enumerate(ORDERS):
            named = dict(zip("abc", axes))
            if after:
                mail.received((s, q, after))
            go(s, q, tag, {named[n]: v for n, v in sel.items()}, named[along])

    for s in WAVES:
        each(s, "a", {"b": 0, "c": 0}, "a")
        each(s, "b0", {"a": 0, "c": 0}, "b")
    each(0, "c0", {"a": 0, "b": 0}, "c")
    for s in WAVES:
        each(s, "b1", {"a": others, "c": 0}, "b", "a")
        if s == 0:
            each(s, "c1", {"a": others, "b": 0}, "c")
    each(0, "c2", {"a": 0, "b": others}, "c", "b0")
    each(0, "c3", {"a": others, "b": others}, "c", "b1")
    each(1, "c0", {"a": 0, "b": 0}, "c")
    each(1, "c1", {"a": others, "b": 0}, "c")
    each(1, "c2", {"a": 0, "b": others}, "c", "b0")
    each(1, "c3", {"a": others, "b": others}, "c", "b1")


def gather_end(buf, out, mail, groups, s):
    for tag in ("c0", "c1", "c2", "c3"):
        for q in range(3):
            mail.received((s, q, tag))

    @pl.loop(0, N)
    def _(i):
        @pl.loop(0, N)
        def _(j):
            for k in range(N):
                for q in range(3):
                    cols = pl.ds(*groups[s][q])
                    out[i * N + j, pl.ds(4 * k, 4), cols] = buf[i, j, k, :, cols]


def rms(wide, gain):
    mean = jnp.mean(wide * wide, axis=-1, keepdims=True)
    return (wide * lax.rsqrt(mean + EPS) * gain).astype(jnp.bfloat16)


def by_tokens(weight, x, groups, s):
    rows = x.shape[0] * x.shape[1]
    total = None
    for q in range(3):
        cols = pl.ds(*groups[s][q])
        part = lax.dot_general(
            weight(cols), x[:, :, cols].reshape(rows, groups[s][q][1]), (((1,), (1,)), ((), ())),
            preferred_element_type=jnp.float32,
        )
        total = part if total is None else total + part
    return total


def order_ids(ids_ref, IDS, Q, V, own):
    Q[...] = jnp.zeros_like(Q)
    Q[0:2, :] = ids_ref[...].astype(jnp.float32)
    V[...] = Q[...].T
    size = ids_ref.shape[1]
    place = lax.broadcasted_iota(jnp.int32, (size, N**3 * 4), 1)
    row = lax.broadcasted_iota(jnp.int32, (size, N**3 * 4), 0)
    chip = jnp.zeros_like(place)
    for n, name in enumerate(AXES):
        chip = chip * N + lax.rem(lax.axis_index(name) + lax.rem(place // (4 * N ** (2 - n)), N), N)
    slot = (lax.axis_index(CORE) * N**3 + chip) * own + lax.rem(place, own)
    value = jnp.where(lax.rem(place, 4) // own == 0, V[:, 0:1], V[:, 1:2])
    IDS[...] = jnp.sum(jnp.where(row == slot, value, 0.0), axis=0, keepdims=True).astype(jnp.int32)


def sort_pairs(n):
    pairs, p = [], 1
    while p < n:
        k = p
        while k >= 1:
            for j in range(k % p, n - k, 2 * k):
                for i in range(min(k, n - j - k)):
                    if (i + j) // (2 * p) == (i + j + k) // (2 * p):
                        pairs.append((i + j, i + j + k))
            k //= 2
        p *= 2
    return pairs


def sort_down(values):
    values = list(values)
    for i, j in sort_pairs(len(values)):
        values[i], values[j] = jnp.maximum(values[i], values[j]), jnp.minimum(values[i], values[j])
    return values


def merge_down(left, right, keep=TOPK):
    left = list(left) + [False] * (keep - len(left))
    right = list(right) + [False] * (keep - len(right))

    def order(u, v):
        if u is None or v is False:
            return u, v
        if v is None or u is False:
            return v, u
        return jnp.maximum(u, v), jnp.minimum(u, v)

    line = [order(left[i], right[keep - 1 - i])[0] for i in range(keep)] + [None] * (32 - keep)
    gap = 16
    while gap:
        for i in range(32):
            if not i & gap:
                line[i], line[i + gap] = order(line[i], line[i + gap])
        gap //= 2
    return line[32 - keep :]


def away(i, j, k):
    offsets = (i, j, k)
    return {name: lax.rem(lax.axis_index(name) + offsets[n], N) for n, name in enumerate(AXES)}


FAR = sorted(
    ((i, j, k) for i in range(N) for j in range(N) for k in range(N)),
    key=lambda at: -sum(min(v, N - v) for v in at),
)


def slot_stats(LT, M, Q, V, IDS, ST, U, mail, columns):
    levels, rows = 16, LT.shape[1]
    deep = LT.shape[0] // levels
    chip = (lax.axis_index("x") * N + lax.axis_index("z")) * N + lax.axis_index("y")
    core = lax.axis_index(CORE)
    first = (core * N**3 + chip) * columns
    second = ((1 - core) * N**3 + chip) * columns
    for t in range(rows // 128):
        lanes = pl.ds(128 * t, 128)
        ids = IDS[:, lanes]

        @pl.loop(0, deep // 16)
        def _(j):
            both = []
            for side in range(2):
                at = pl.multiple_of(side * (deep // 2) + j * 8, 8)
                both.append(sort_down([LT[pl.ds(l * deep + at, 8), lanes] for l in range(levels)]))
            for l, value in enumerate(merge_down(*both)):
                M[l, pl.ds(pl.multiple_of(j * 8, 8), 8), lanes] = value

        have = deep // 16
        while have > 1:
            have //= 2

            @pl.loop(0, have)
            def _(j):
                both = []
                for side in range(2):
                    at = pl.multiple_of((side * have + j) * 8, 8)
                    both.append([M[l, pl.ds(at, 8), lanes] for l in range(TOPK)])
                for l, value in enumerate(merge_down(*both)):
                    M[l, pl.ds(pl.multiple_of(j * 8, 8), 8), lanes] = value

        top = [M[l, pl.ds(0, 8), lanes] for l in range(TOPK)]
        for shift in (4, 2, 1):
            top = merge_down(top, [pltpu.roll(v, shift, 0) for v in top])
        peak = top[0]

        def body(j, carry):
            total, hit = carry
            at = pl.multiple_of(j * 8, 8)
            value = LT[pl.ds(at, 8), lanes]
            row = lax.broadcasted_iota(jnp.int32, (8, 128), 0) + at
            late = row >= LT.shape[0] // 2
            column = jnp.where(late, row - LT.shape[0] // 2, row)
            token = column + jnp.where(late, second, first)
            same = (token == ids) & (column < columns)
            return total + jnp.exp(value - peak), hit + jnp.where(same, value, 0.0)

        zero = jnp.zeros((8, 128), jnp.float32)
        total, hit = lax.fori_loop(0, LT.shape[0] // 8, body, (zero, zero), unroll=8)
        for l in range(TOPK):
            Q[pl.ds(l, 1), lanes] = top[l][0:1]
        Q[pl.ds(TOPK, 1), lanes] = jnp.sum(total, axis=0, keepdims=True)
        Q[pl.ds(TOPK + 1, 1), lanes] = jnp.sum(hit, axis=0, keepdims=True)
        V[lanes, :] = Q[:, lanes].T
        for at in FAR:
            i, j, k = at
            if (i * N**2 + j * N + k) * 4 // 128 == t:
                to = U if at == (0, 0, 0) else ST
                to[i, j, k] = V[pl.ds(((i * N + j) * N + k) * 4, 4), :]
        for at in FAR[:-1]:
            i, j, k = at
            if (i * N**2 + j * N + k) * 4 // 128 == t:
                mail.send(0, ST.at[i, j, k], U.at[(N - i) % N, (N - j) % N, (N - k) % N], away(i, j, k))


def merged(U, V, Q):
    for i in range(N):
        for j in range(N):
            for k in range(N):
                V[pl.ds(((i * N + j) * N + k) * 4, 4), :] = U[i, j, k]
    Q[...] = V[...].T

    def line(l):
        return [Q[pl.ds(l, 1), pl.ds(128 * t, 128)] for t in range(2)]

    lists = [line(l) for l in range(TOPK)]
    top = merge_down([v[0] for v in lists], [v[1] for v in lists])
    for shift in (64, 32, 16, 8, 4):
        top = merge_down(top, [pltpu.roll(v, shift, 1) for v in top])
    peak = top[0]
    sums, hits = line(TOPK), line(TOPK + 1)
    total = sum(s * jnp.exp(v - peak) for s, v in zip(sums, lists[0]))
    hit = hits[0] + hits[1]
    for shift in (64, 32, 16, 8, 4):
        total = total + pltpu.roll(total, shift, 1)
        hit = hit + pltpu.roll(hit, shift, 1)
    log_norm = peak + jnp.log(total)
    mass = sum(jnp.exp(v - log_norm) for v in top)
    return hit - log_norm, log_norm, mass


def by_sequence(logprob, sid_ref):
    lane = lax.broadcasted_iota(jnp.int32, (1, 128), 1)
    turned = [logprob] + [pltpu.roll(logprob, j, 1) for j in (1, 2, 3)]
    part = jnp.zeros((1, 128), jnp.float32)
    for t in range(4):
        spread = turned[0]
        for j in (1, 2, 3):
            spread = jnp.where(lax.rem(lane - t + 4, 4) == j, turned[j], spread)
        mine = (lane // SEQS == t // 2) & (lax.rem(lane, SEQS) == sid_ref[t // 2, t % 2])
        part = part + jnp.where(mine, spread, 0.0)
    return part


def score_kernel(
    h_ref, gf_ref, gl_ref, wg_ref, wu_ref, wd_ref, hw_ref, ids_ref, sid_ref,
    out_ref,
    HS, G, X, S, R1, R2, R3, T1, T2, F, PB, W, WD, Y, ACT, HB, LT, M, Q, V, IDS, ST, U, A, B,
    own_s, swap_s, swap_r, g_s, g_r, r_s, r_r, g2_s, g2_r, a_s, a_r, q_s, q_r,
):
    width = h_ref.shape[-1]
    groups = column_groups(width)
    rows = N**3 * 4
    hidden = W.shape[1]
    columns = HB.shape[1]
    loads = []
    for n, (src, dst) in enumerate(((wg_ref, W.at[0]), (wu_ref, W.at[1]), (wd_ref, WD.at[0]))):
        copy = pltpu.make_async_copy(src, dst, own_s.at[n])
        copy.start()
        loads.append(copy)
    greet()
    own = h_ref.shape[1]
    for m in range(h_ref.shape[0]):
        HS[pl.ds(m * own, own), :] = h_ref[m].astype(jnp.float32)
    G[0, 0, 0] = rms(HS[...], gf_ref[...])
    met()
    mail = Mail(g_s, g_r)
    swap = Mail(swap_s, swap_r)
    for tag, src, dst in (("g", wg_ref, W.at[2]), ("u", wu_ref, W.at[3]), ("d", wd_ref, WD.at[1])):
        swap.send(tag, src, dst, partner())
    gather_start(G, mail, groups)
    order_ids(ids_ref, IDS, Q, V, own)
    for copy in loads[:2]:
        copy.wait()
    for tag in ("g", "u"):
        swap.received(tag)
    for s in WAVES:
        gather_end(G, X, mail, groups, s)
        part = by_tokens(lambda cols: W[:, :, cols].reshape(4 * hidden, cols.size), X, groups, s)
        Y[...] = part if s == 0 else Y[...] + part
    loads[2].wait()
    swap.received("d")
    swap.send("h", hw_ref, HB.at[1], partner())
    own_head = pltpu.make_async_copy(hw_ref, HB.at[0], own_s.at[3])
    own_head.start()
    acts = []
    for p in range(2):
        gate, up = Y[pl.ds(2 * p * hidden, hidden), :], Y[pl.ds((2 * p + 1) * hidden, hidden), :]
        acts.append(gate / (1.0 + jnp.exp(-gate)) * up)
    ACT[...] = jnp.concatenate(acts, axis=0).T.astype(jnp.bfloat16)
    mail.all_sent()

    red = Mail(r_s, r_r)

    def down(at, size):
        cols = pl.ds(at, size)
        part = jnp.dot(ACT[...], WD[:, :, cols].reshape(2 * hidden, size), preferred_element_type=jnp.float32)
        PB[:, :, pl.ds(0, size)] = part.astype(jnp.bfloat16).reshape(N * N, N * 4, size)
        for i in range(N):
            for j in range(N):
                for k in range(N):
                    S[i, j, k, :, cols] = PB[i * N + j, pl.ds(4 * k, 4), pl.ds(0, size)]

    every = [(s, q, pl.ds(*groups[s][q])) + ORDERS[q] for s in WAVES for q in range(3)]
    for s, q, cols, a, b, c in every:
        start, size = groups[s][q]

        down(start, size)
        rest = (slice(None), cols)
        for k in (2, 1, 3):
            red.send((s, q, 1), S.at[pick({c: k}) + rest], R1.at[(k - 1, slice(None), slice(None)) + rest], toward(c, k))
    for s, q, cols, a, b, c in every:
        red.received((s, q, 1))

        @pl.loop(0, N)
        def _(i):
            @pl.loop(0, N)
            def _(j):
                left = [i, j]
                sel = {ax: left.pop(0) for ax in range(3) if ax != c}
                sel[c] = 0
                total = S[pick(sel) + (slice(None), cols)].astype(jnp.float32)
                for k in range(3):
                    total += R1[k, i, j, :, cols].astype(jnp.float32)
                T1[i, j, :, cols] = total.astype(jnp.bfloat16)

        first = min(a, b)
        for k in (2, 1, 3):
            src = T1.at[k, :, :, cols] if b == first else T1.at[:, k, :, cols]
            red.send((s, q, 2), src, R2.at[k - 1, :, :, cols], toward(b, k))
    for s, q, cols, a, b, c in every:
        red.received((s, q, 2))
        first = min(a, b)
        for i in range(N):
            total = (T1[0, i, :, cols] if b == first else T1[i, 0, :, cols]).astype(jnp.float32)
            for k in range(3):
                total += R2[k, i, :, cols].astype(jnp.float32)
            T2[i, :, cols] = total.astype(jnp.bfloat16)
        for k in (2, 1, 3):
            red.send((s, q, 3), T2.at[k, :, cols], R3.at[k - 1, :, cols], toward(a, k))
    for s, q, cols, a, b, c in every:
        red.received((s, q, 3))
        total = T2[0, :, cols].astype(jnp.float32)
        for k in range(3):
            total += R3[k, :, cols].astype(jnp.float32)
        F[:, cols] = total

    residual = (HS[...] + F[...]).astype(jnp.bfloat16)
    G[0, 0, 0] = rms(residual.astype(jnp.float32), gl_ref[...])
    mail2 = Mail(g2_s, g2_r)
    gather_start(G, mail2, groups)
    swap.received("h")
    own_head.wait()
    half, tall = LT.shape[0] // 2, 512
    for s in WAVES:
        gather_end(G, X, mail2, groups, s)
        for p in range(2):
            if s == 0:
                LT[pl.ds(p * half + columns // 8 * 8, half - columns // 8 * 8), :] = jnp.full(
                    (half - columns // 8 * 8, rows), NEG, jnp.float32
                )

            def logits(at, size):
                part = by_tokens(lambda cols: HB[p, pl.ds(at, size), cols], X, groups, s)
                to = pl.ds(p * half + at, size)
                LT[to, :] = part if s == 0 else LT[to, :] + part

            for at in range(0, columns, tall):
                logits(at, min(tall, columns - at))

    stats = Mail(a_s, a_r)
    slot_stats(LT, M, Q, V, IDS, ST, U, stats, columns)
    stats.received(0)
    logprob, log_norm, mass = merged(U, V, Q)

    A[0] = by_sequence(logprob, sid_ref)
    seq = Mail(q_s, q_r)
    seq.send(0, A.at[0], A.at[1], partner())
    seq.received(0)
    B[0, 0, 0] = A[0] + A[1]
    for i, j, k in FAR[:-1]:
        seq.send(1, B.at[0, 0, 0], B.at[(N - i) % N, (N - j) % N, (N - k) % N], away(i, j, k))
    seq.received(1)

    def joined(values):
        return (values[0] + values[2]) + (values[1] + values[3])

    both = joined([joined([joined([B[i, j, k] for i in range(N)]) for j in range(N)]) for k in range(N)])
    for n, value in enumerate((logprob, log_norm, mass, both)):
        out_ref[pl.ds(n, 1), :] = value
    out_ref[4:8, :] = jnp.zeros((4, 128), jnp.float32)
    for m in (swap, red, mail2, stats, seq):
        m.all_sent()


def score(h, gain_ffn, gain_final, w_gate, w_up, w_down, head, ids, seq_ids):
    hidden, width = w_gate.shape
    columns = head.shape[0]
    half = -(-columns // 256) * 256
    rows = N**3 * 4
    bf16, f32 = jnp.bfloat16, jnp.float32
    vmem, anywhere = pl.BlockSpec(memory_space=pltpu.VMEM), pl.BlockSpec(memory_space=pl.ANY)
    dma = lambda n: pltpu.SemaphoreType.DMA((n,))
    stat = pltpu.VMEM((N, N, N, 4, 128), f32)
    return pl.pallas_call(
        score_kernel,
        out_shape=jax.ShapeDtypeStruct((8, 128), f32),
        in_specs=[vmem, vmem, vmem, anywhere, anywhere, anywhere, anywhere, vmem, pl.BlockSpec(memory_space=pltpu.SMEM)],
        out_specs=vmem,
        scratch_shapes=[
            pltpu.VMEM((4, width), f32),
            pltpu.VMEM((N, N, N, 4, width), bf16),
            pltpu.VMEM((N * N, N * 4, width), bf16),
            pltpu.VMEM((N, N, N, 4, width), bf16),
            pltpu.VMEM((3, N, N, 4, width), bf16),
            pltpu.VMEM((3, N, 4, width), bf16),
            pltpu.VMEM((3, 4, width), bf16),
            pltpu.VMEM((N, N, 4, width), bf16),
            pltpu.VMEM((N, 4, width), bf16),
            pltpu.VMEM((4, width), f32),
            pltpu.VMEM((N * N, N * 4, 1280), bf16),
            pltpu.VMEM((4, hidden, width), bf16),
            pltpu.VMEM((2, hidden, width), bf16),
            pltpu.VMEM((4 * hidden, rows), f32),
            pltpu.VMEM((rows, 2 * hidden), bf16),
            pltpu.VMEM((2, columns, width), bf16),
            pltpu.VMEM((2 * half, rows), f32),
            pltpu.VMEM((TOPK, half // 16, rows), f32),
            pltpu.VMEM((128, rows), f32),
            pltpu.VMEM((rows, 128), f32),
            pltpu.VMEM((1, rows), jnp.int32),
            stat, stat,
            pltpu.VMEM((2, 1, 128), f32),
            pltpu.VMEM((N, N, N, 1, 128), f32),
            dma(4), dma(4), dma(4), dma(126), dma(126), dma(54), dma(54), dma(126), dma(126), dma(63), dma(63), dma(64), dma(64),
        ],
        compiler_params=pltpu.CompilerParams(collective_id=0, has_side_effects=True, vmem_limit_bytes=67043328),
        name="score",
    )(h, gain_ffn, gain_final, w_gate, w_up, w_down, head, ids, seq_ids)


def emit_kernel(x_ref, lp_ref, ln_ref, tm_ref, sq_ref):
    for n, ref in enumerate((lp_ref, ln_ref, tm_ref, sq_ref)):
        size = ref.shape[1]
        line = x_ref[pl.ds(n, 1), :]
        ref[0:1, :] = line[:, 0:size]
        ref[1:2, :] = pltpu.roll(line, 128 - size, 1)[:, 0:size]


def emit(x, own):
    f32 = jnp.float32
    small = jax.ShapeDtypeStruct((2, own), f32)
    return pl.pallas_call(
        emit_kernel, out_shape=(small, small, small, jax.ShapeDtypeStruct((2, SEQS), f32)), name="emit"
    )(x)


def body(hidden_in, gain_ffn, w_gate, w_up, w_down, gain_final, head_weight, sampled_ids, seq_ids):
    width = hidden_in.shape[-1]
    packed = score(
        hidden_in, gain_ffn.reshape(1, width), gain_final.reshape(1, width),
        w_gate.T, w_up.T, w_down, head_weight.T, sampled_ids, seq_ids,
    )
    return tuple(emit(packed, hidden_in.shape[1]))


def solution(mesh):
    split = Mesh(mesh.devices.reshape(mesh.shape["section"], N, N, N), EVERY)
    rows = P(None, EVERY)
    return jax.shard_map(
        body,
        mesh=split,
        in_specs=(P(None, EVERY, None), P(), rows, rows, P(EVERY, None), P(), rows, P(), rows),
        out_specs=(rows, rows, rows, P()),
        check_vma=False,
    )
```

```python
import functools

import jax
import jax.numpy as jnp
from jax import lax
from jax.experimental import pallas as pl
from jax.experimental.pallas import tpu as pltpu
from jax.sharding import Mesh
from jax.sharding import PartitionSpec as P

SEQS = 8
TOPK = 20
EPS = 1e-06
NEG = -3.0e38
MESH = pl.DeviceIdType.MESH
CORE = "section"
AXES = ("x", "z", "y")
EVERY = (CORE,) + AXES
ORDERS = ((0, 1, 2), (1, 2, 0), (2, 0, 1))
N = 4


def pick(sel):
    return tuple(sel.get(i, slice(None)) for i in range(3))


def column_groups(width):
    tiles = width // 128
    cuts = [0, (tiles + 2) // 3, (2 * tiles + 2) // 3, tiles]
    waves = [[], []]
    for q in range(3):
        size = cuts[q + 1] - cuts[q]
        half = (size + 1) // 2 if q < 2 else size // 2 - (size // 2) % 2
        at = 128 * cuts[q]
        waves[0].append((at, 128 * half))
        waves[1].append((at + 128 * half, 128 * (size - half)))
    return waves


def toward(axis, k):
    name = AXES[axis]
    return {name: lax.rem(lax.axis_index(name) + k, N)}


def partner():
    return {CORE: 1 - lax.axis_index(CORE)}


def away(i, j, k):
    offsets = (i, j, k)
    return {name: lax.rem(lax.axis_index(name) + offsets[n], N) for n, name in enumerate(AXES)}


FAR = sorted(
    ((i, j, k) for i in range(N) for j in range(N) for k in range(N)),
    key=lambda at: -sum(min(v, N - v) for v in at),
)


def greet():
    barrier = pltpu.get_barrier_semaphore()
    for axis in range(3):
        for k in (1, 2, 3):
            pl.semaphore_signal(barrier, inc=1, device_id=toward(axis, k), device_id_type=MESH)
    pl.semaphore_signal(barrier, inc=1, device_id=partner(), device_id_type=MESH)


def met():
    pl.semaphore_wait(pltpu.get_barrier_semaphore(), 10)


class Mail:
    def __init__(self, send_sem, recv_sem):
        self.send_sem, self.recv_sem = send_sem, recv_sem
        self.wholes, self.places = {}, {}

    def send(self, tag, whole, src, dst, device):
        place = self.places.setdefault(tag, len(self.places))
        self.wholes[tag] = whole
        pltpu.make_async_remote_copy(
            src_ref=src,
            dst_ref=dst,
            send_sem=self.send_sem.at[place],
            recv_sem=self.recv_sem.at[place],
            device_id=device,
            device_id_type=MESH,
        ).start()

    def all_of(self, tag):
        place, whole = self.places[tag], self.wholes[tag]
        return pltpu.make_async_remote_copy(
            src_ref=whole,
            dst_ref=whole,
            send_sem=self.send_sem.at[place],
            recv_sem=self.recv_sem.at[place],
            device_id=partner(),
            device_id_type=MESH,
        )

    def received(self, tag):
        self.all_of(tag).wait_recv()

    def all_sent(self):
        for tag in self.places:
            self.all_of(tag).wait_send()

    def spread(self, src, dst, only=None):
        some = pl.ds(1, 3)
        wholes = (dst.at[some], dst.at[0, some], dst.at[0, 0, some])
        for at in FAR[:-1]:
            if only is None or only(at):
                tag = 0 if at[0] else 1 if at[1] else 2
                self.send(tag, wholes[tag], src(*at), dst.at[tuple((N - v) % N for v in at)], away(*at))

    def all_received(self):
        for tag in self.places:
            self.received(tag)


WAVES = (0, 1)


class Gather:
    def __init__(self, buf, mail, groups):
        self.buf, self.mail, self.groups = buf, mail, groups

    def each(self, s, tag, sel, along, after=None):
        for q, axes in enumerate(ORDERS):
            named = dict(zip("abc", axes))
            axis = named[along]
            if after:
                self.mail.received((s, q, after))
            rest = (slice(None), pl.ds(*self.groups[s][q]))

            def part(at):
                return self.buf.at[pick({**{named[n]: v for n, v in sel.items()}, axis: at}) + rest]

            for k in (1, 3, 2):
                self.mail.send((s, q, tag), part(pl.ds(1, 3)), part(0), part(N - k), toward(axis, k))

    def open(self, s):
        self.each(s, "a", {"b": 0, "c": 0}, "a")
        self.each(s, "b0", {"a": 0, "c": 0}, "b")
        if s == 0:
            self.each(0, "c0", {"a": 0, "b": 0}, "c")

    def relay(self):
        others = pl.ds(1, 3)
        for s in WAVES:
            self.each(s, "b1", {"a": others, "c": 0}, "b", "a")
            if s == 0:
                self.each(s, "c1", {"a": others, "b": 0}, "c")
        self.each(0, "c2", {"a": 0, "b": others}, "c", "b0")
        self.each(0, "c3", {"a": others, "b": others}, "c", "b1")
        self.each(1, "c0", {"a": 0, "b": 0}, "c")
        self.each(1, "c1", {"a": others, "b": 0}, "c")
        self.each(1, "c2", {"a": 0, "b": others}, "c", "b0")
        self.each(1, "c3", {"a": others, "b": others}, "c", "b1")


def gather_end(buf, out, mail, groups, s):
    for tag in ("c0", "c1", "c2", "c3"):
        for q in range(3):
            mail.received((s, q, tag))

    @pl.loop(0, N)
    def _(i):
        @pl.loop(0, N)
        def _(j):
            for k in range(N):
                for q in range(3):
                    cols = pl.ds(*groups[s][q])
                    out[i * N + j, pl.ds(4 * k, 4), cols] = buf[i, j, k, :, cols]


def rms(wide, gain):
    mean = jnp.mean(wide * wide, axis=-1, keepdims=True)
    return (wide * lax.rsqrt(mean + EPS) * gain).astype(jnp.bfloat16)


def by_tokens(weight, x, groups, s):
    rows = x.shape[0] * x.shape[1]
    total = None
    for q in range(3):
        cols = pl.ds(*groups[s][q])
        part = lax.dot_general(
            weight(cols), x[:, :, cols].reshape(rows, groups[s][q][1]), (((1,), (1,)), ((), ())),
            preferred_element_type=jnp.float32,
        )
        total = part if total is None else total + part
    return total


def order_ids(ids_ref, IDS, Q, V, own):
    Q[...] = jnp.zeros_like(Q)
    Q[0:2, :] = ids_ref[...].astype(jnp.float32)
    V[...] = Q[...].T
    size = ids_ref.shape[1]
    place = lax.broadcasted_iota(jnp.int32, (size, N**3 * 4), 1)
    row = lax.broadcasted_iota(jnp.int32, (size, N**3 * 4), 0)
    chip = jnp.zeros_like(place)
    for n, name in enumerate(AXES):
        chip = chip * N + lax.rem(lax.axis_index(name) + lax.rem(place // (4 * N ** (2 - n)), N), N)
    slot = (lax.axis_index(CORE) * N**3 + chip) * own + lax.rem(place, own)
    value = jnp.where(lax.rem(place, 4) // own == 0, V[:, 0:1], V[:, 1:2])
    IDS[...] = jnp.sum(jnp.where(row == slot, value, 0.0), axis=0, keepdims=True).astype(jnp.int32)


def sort_pairs(n):
    pairs, p = [], 1
    while p < n:
        k = p
        while k >= 1:
            for j in range(k % p, n - k, 2 * k):
                for i in range(min(k, n - j - k)):
                    if (i + j) // (2 * p) == (i + j + k) // (2 * p):
                        pairs.append((i + j, i + j + k))
            k //= 2
        p *= 2
    return pairs


def sort_down(values):
    values = list(values)
    for i, j in sort_pairs(len(values)):
        values[i], values[j] = jnp.maximum(values[i], values[j]), jnp.minimum(values[i], values[j])
    return values


def merge_down(left, right, keep=TOPK):
    left = list(left) + [False] * (keep - len(left))
    right = list(right) + [False] * (keep - len(right))

    def order(u, v):
        if u is None or v is False:
            return u, v
        if v is None or u is False:
            return v, u
        return jnp.maximum(u, v), jnp.minimum(u, v)

    line = [order(left[i], right[keep - 1 - i])[0] for i in range(keep)] + [None] * (32 - keep)
    gap = 16
    while gap:
        for i in range(32):
            if not i & gap:
                line[i], line[i + gap] = order(line[i], line[i + gap])
        gap //= 2
    return line[32 - keep :]


def row_factors(C):
    lane = lax.broadcasted_iota(jnp.int32, (1, N**3 * 4), 1)
    total = jnp.zeros((1, N**3 * 4), jnp.float32)
    for i in range(N):
        for j in range(N):
            for k in range(N):
                line = jnp.concatenate([C[i, j, k]] * (N**3 * 4 // 128), axis=1)
                total = total + jnp.where(lane // 4 == (i * N + j) * N + k, line, 0.0)
    return total


def slot_stats(LT, M, Q, V, IDS, ST, U, mail, columns):
    levels, rows = 16, LT.shape[1]
    deep = LT.shape[0] // levels
    chip = (lax.axis_index("x") * N + lax.axis_index("z")) * N + lax.axis_index("y")
    core = lax.axis_index(CORE)
    first = (core * N**3 + chip) * columns
    second = ((1 - core) * N**3 + chip) * columns
    for t in range(rows // 128):
        lanes = pl.ds(128 * t, 128)
        ids = IDS[:, lanes]

        @pl.loop(0, deep // 16)
        def _(j):
            both = []
            for side in range(2):
                at = pl.multiple_of(side * (deep // 2) + j * 8, 8)
                both.append(sort_down([LT[pl.ds(l * deep + at, 8), lanes] for l in range(levels)]))
            for l, value in enumerate(merge_down(*both)):
                M[l, pl.ds(pl.multiple_of(j * 8, 8), 8), lanes] = value

        have = deep // 16
        while have > 1:
            have //= 2

            @pl.loop(0, have)
            def _(j):
                both = []
                for side in range(2):
                    at = pl.multiple_of((side * have + j) * 8, 8)
                    both.append([M[l, pl.ds(at, 8), lanes] for l in range(TOPK)])
                for l, value in enumerate(merge_down(*both)):
                    M[l, pl.ds(pl.multiple_of(j * 8, 8), 8), lanes] = value

        top = [M[l, pl.ds(0, 8), lanes] for l in range(TOPK)]
        for shift in (4, 2, 1):
            top = merge_down(top, [pltpu.roll(v, shift, 0) for v in top])
        peak = top[0]

        def body(j, carry):
            total, hit = carry
            at = pl.multiple_of(j * 8, 8)
            value = LT[pl.ds(at, 8), lanes]
            row = lax.broadcasted_iota(jnp.int32, (8, 128), 0) + at
            late = row >= LT.shape[0] // 2
            column = jnp.where(late, row - LT.shape[0] // 2, row)
            token = column + jnp.where(late, second, first)
            same = (token == ids) & (column < columns)
            return total + jnp.exp(value - peak), hit + jnp.where(same, value, 0.0)

        zero = jnp.zeros((8, 128), jnp.float32)
        total, hit = lax.fori_loop(0, LT.shape[0] // 8, body, (zero, zero), unroll=8)
        for l in range(TOPK):
            Q[pl.ds(l, 1), lanes] = top[l][0:1]
        Q[pl.ds(TOPK, 1), lanes] = jnp.sum(total, axis=0, keepdims=True)
        Q[pl.ds(TOPK + 1, 1), lanes] = jnp.sum(hit, axis=0, keepdims=True)
        V[lanes, :] = Q[:, lanes].T
        for at in FAR:
            i, j, k = at
            if (i * N**2 + j * N + k) * 4 // 128 == t:
                to = U if at == (0, 0, 0) else ST
                to[i, j, k] = V[pl.ds(((i * N + j) * N + k) * 4, 4), :]
        mail.spread(lambda *at: ST.at[at], U, lambda at: (at[0] * N**2 + at[1] * N + at[2]) * 4 // 128 == t)


def merged(U, V, Q):
    for i in range(N):
        for j in range(N):
            for k in range(N):
                V[pl.ds(((i * N + j) * N + k) * 4, 4), :] = U[i, j, k]
    Q[...] = V[...].T

    def line(l):
        return [Q[pl.ds(l, 1), pl.ds(128 * t, 128)] for t in range(2)]

    lists = [line(l) for l in range(TOPK)]
    top = merge_down([v[0] for v in lists], [v[1] for v in lists])
    for shift in (64, 32, 16, 8, 4):
        top = merge_down(top, [pltpu.roll(v, shift, 1) for v in top])
    peak = top[0]
    sums, hits = line(TOPK), line(TOPK + 1)
    total = sum(s * jnp.exp(v - peak) for s, v in zip(sums, lists[0]))
    hit = hits[0] + hits[1]
    for shift in (64, 32, 16, 8, 4):
        total = total + pltpu.roll(total, shift, 1)
        hit = hit + pltpu.roll(hit, shift, 1)
    log_norm = peak + jnp.log(total)
    mass = sum(jnp.exp(v - log_norm) for v in top)
    return hit - log_norm, log_norm, mass


def by_sequence(logprob, sid_ref):
    lane = lax.broadcasted_iota(jnp.int32, (1, 128), 1)
    turned = [logprob] + [pltpu.roll(logprob, j, 1) for j in (1, 2, 3)]
    part = jnp.zeros((1, 128), jnp.float32)
    for t in range(4):
        spread = turned[0]
        for j in (1, 2, 3):
            spread = jnp.where(lax.rem(lane - t + 4, 4) == j, turned[j], spread)
        mine = (lane // SEQS == t // 2) & (lax.rem(lane, SEQS) == sid_ref[t // 2, t % 2])
        part = part + jnp.where(mine, spread, 0.0)
    return part


def score_kernel(
    h_ref, gf_ref, gl_ref, wg_ref, wu_ref, wd_ref, hw_ref, ids_ref, sid_ref,
    out_ref,
    HS, G, X, S, R1, R2, R3, T1, T2, PB, W, WD, Y, ACT, HB, LT, M, Q, V, IDS, ST, U, A, B, C, FS,
    own_s, swap_s, swap_r, g_s, g_r, r_s, r_r, g2_s, g2_r, a_s, a_r, q_s, q_r, c_s, c_r,
):
    width = h_ref.shape[-1]
    groups = column_groups(width)
    rows = N**3 * 4
    hidden = W.shape[1]
    columns = HB.shape[1]
    loads = []
    for n, (src, dst) in enumerate(((wg_ref, W.at[0]), (wu_ref, W.at[1]), (wd_ref, WD.at[0]))):
        copy = pltpu.make_async_copy(src, dst, own_s.at[n])
        copy.start()
        loads.append(copy)
    greet()
    own = h_ref.shape[1]
    for m in range(h_ref.shape[0]):
        HS[pl.ds(m * own, own), :] = h_ref[m].astype(jnp.float32)
    G[0, 0, 0] = rms(HS[...], gf_ref[...])
    met()
    mail = Mail(g_s, g_r)
    swap = Mail(swap_s, swap_r)
    for tag, src, dst in (("g", wg_ref, W.at[2]), ("u", wu_ref, W.at[3]), ("d", wd_ref, WD.at[1])):
        swap.send(tag, dst, src, dst, partner())
    gather = Gather(G, mail, groups)
    for s in WAVES:
        gather.open(s)
    gather.relay()
    order_ids(ids_ref, IDS, Q, V, own)
    for copy in loads[:2]:
        copy.wait()
    for tag in ("g", "u"):
        swap.received(tag)
    for s in WAVES:
        gather_end(G, X, mail, groups, s)
        part = by_tokens(lambda cols: W[:, :, cols].reshape(4 * hidden, cols.size), X, groups, s)
        Y[...] = part if s == 0 else Y[...] + part
    loads[2].wait()
    swap.received("d")
    swap.send("h", HB.at[1], hw_ref, HB.at[1], partner())
    own_head = pltpu.make_async_copy(hw_ref, HB.at[0], own_s.at[3])
    own_head.start()
    acts = []
    for p in range(2):
        gate, up = Y[pl.ds(2 * p * hidden, hidden), :], Y[pl.ds((2 * p + 1) * hidden, hidden), :]
        acts.append(gate / (1.0 + jnp.exp(-gate)) * up)
    ACT[...] = jnp.concatenate(acts, axis=0).T.astype(jnp.bfloat16)
    mail.all_sent()

    red = Mail(r_s, r_r)

    def down(at, size):
        cols = pl.ds(at, size)
        part = jnp.dot(ACT[...], WD[:, :, cols].reshape(2 * hidden, size), preferred_element_type=jnp.float32)
        PB[:, :, pl.ds(0, size)] = part.astype(jnp.bfloat16).reshape(N * N, N * 4, size)
        for i in range(N):
            for j in range(N):
                for k in range(N):
                    S[i, j, k, :, cols] = PB[i * N + j, pl.ds(4 * k, 4), pl.ds(0, size)]

    every = [(s, q, pl.ds(*groups[s][q])) + ORDERS[q] for s in WAVES for q in range(3)]
    for s, q, cols, a, b, c in every:
        start, size = groups[s][q]

        down(start, size)
        rest = (slice(None), cols)
        for k in (2, 1, 3):
            whole = R1.at[:, :, :, :, cols]
            red.send((s, q, 1), whole, S.at[pick({c: k}) + rest], R1.at[k - 1, :, :, :, cols], toward(c, k))
    for s, q, cols, a, b, c in every:
        red.received((s, q, 1))

        @pl.loop(0, N)
        def _(i):
            @pl.loop(0, N)
            def _(j):
                left = [i, j]
                sel = {ax: left.pop(0) for ax in range(3) if ax != c}
                sel[c] = 0
                total = S[pick(sel) + (slice(None), cols)].astype(jnp.float32)
                for k in range(3):
                    total += R1[k, i, j, :, cols].astype(jnp.float32)
                T1[i, j, :, cols] = total.astype(jnp.bfloat16)

        first = min(a, b)
        for k in (2, 1, 3):
            src = T1.at[k, :, :, cols] if b == first else T1.at[:, k, :, cols]
            red.send((s, q, 2), R2.at[:, :, :, cols], src, R2.at[k - 1, :, :, cols], toward(b, k))
    for s, q, cols, a, b, c in every:
        red.received((s, q, 2))
        first = min(a, b)
        for i in range(N):
            total = (T1[0, i, :, cols] if b == first else T1[i, 0, :, cols]).astype(jnp.float32)
            for k in range(3):
                total += R2[k, i, :, cols].astype(jnp.float32)
            T2[i, :, cols] = total.astype(jnp.bfloat16)
        for k in (2, 1, 3):
            red.send((s, q, 3), R3.at[:, :, cols], T2.at[k, :, cols], R3.at[k - 1, :, cols], toward(a, k))
    mail2 = Mail(g2_s, g2_r)
    gather = Gather(G, mail2, groups)
    squares = jnp.zeros((4, 1), jnp.float32)
    for s in WAVES:
        for q in range(3):
            cols = pl.ds(*groups[s][q])
            red.received((s, q, 3))
            total = T2[0, :, cols].astype(jnp.float32)
            for k in range(3):
                total += R3[k, :, cols].astype(jnp.float32)
            residual = (HS[:, cols] + total).astype(jnp.bfloat16).astype(jnp.float32)
            squares += jnp.sum(residual * residual, axis=-1, keepdims=True)
            G[0, 0, 0, :, cols] = (residual * gl_ref[:, cols]).astype(jnp.bfloat16)
        gather.open(s)
    factor = jnp.broadcast_to(lax.rsqrt(squares / width + EPS), (4, 128))
    turn = lax.rem(lax.broadcasted_iota(jnp.int32, (4, 128), 1), 4) == lax.broadcasted_iota(jnp.int32, (4, 128), 0)
    C[0, 0, 0] = jnp.sum(jnp.where(turn, factor, 0.0), axis=0, keepdims=True)
    gather.relay()
    scales = Mail(c_s, c_r)
    scales.spread(lambda *at: C.at[0, 0, 0], C)
    swap.received("h")
    own_head.wait()
    half, tall = LT.shape[0] // 2, 512
    for s in WAVES:
        gather_end(G, X, mail2, groups, s)
        if s == WAVES[-1]:
            scales.all_received()
            FS[...] = row_factors(C)
        for p in range(2):
            if s == 0:
                LT[pl.ds(p * half + columns // 8 * 8, half - columns // 8 * 8), :] = jnp.full(
                    (half - columns // 8 * 8, rows), NEG, jnp.float32
                )

            def logits(at, size):
                part = by_tokens(lambda cols: HB[p, pl.ds(at, size), cols], X, groups, s)
                to = pl.ds(p * half + at, size)
                LT[to, :] = part if s == 0 else (LT[to, :] + part) * FS[...]

            for at in range(0, columns, tall):
                logits(at, min(tall, columns - at))

    stats = Mail(a_s, a_r)
    slot_stats(LT, M, Q, V, IDS, ST, U, stats, columns)
    stats.all_received()
    logprob, log_norm, mass = merged(U, V, Q)

    A[0] = by_sequence(logprob, sid_ref)
    seq = Mail(q_s, q_r)
    swap.send("s", A.at[1], A.at[0], A.at[1], partner())
    swap.received("s")
    B[0, 0, 0] = A[0] + A[1]
    seq.spread(lambda *at: B.at[0, 0, 0], B)
    seq.all_received()

    def joined(values):
        return (values[0] + values[2]) + (values[1] + values[3])

    both = joined([joined([joined([B[i, j, k] for i in range(N)]) for j in range(N)]) for k in range(N)])
    for n, value in enumerate((logprob, log_norm, mass, both)):
        out_ref[pl.ds(n, 1), :] = value
    out_ref[4:8, :] = jnp.zeros((4, 128), jnp.float32)
    for m in (swap, red, mail2, scales, stats, seq):
        m.all_sent()


def score(h, gain_ffn, gain_final, w_gate, w_up, w_down, head, ids, seq_ids):
    hidden, width = w_gate.shape
    columns = head.shape[0]
    half = -(-columns // 256) * 256
    rows = N**3 * 4
    bf16, f32 = jnp.bfloat16, jnp.float32
    vmem, anywhere = pl.BlockSpec(memory_space=pltpu.VMEM), pl.BlockSpec(memory_space=pl.ANY)
    dma = lambda n: pltpu.SemaphoreType.DMA((n,))
    stat = pltpu.VMEM((N, N, N, 4, 128), f32)
    return pl.pallas_call(
        score_kernel,
        out_shape=jax.ShapeDtypeStruct((8, 128), f32),
        in_specs=[vmem, vmem, vmem, anywhere, anywhere, anywhere, anywhere, vmem, pl.BlockSpec(memory_space=pltpu.SMEM)],
        out_specs=vmem,
        scratch_shapes=[
            pltpu.VMEM((4, width), f32),
            pltpu.VMEM((N, N, N, 4, width), bf16),
            pltpu.VMEM((N * N, N * 4, width), bf16),
            pltpu.VMEM((N, N, N, 4, width), bf16),
            pltpu.VMEM((3, N, N, 4, width), bf16),
            pltpu.VMEM((3, N, 4, width), bf16),
            pltpu.VMEM((3, 4, width), bf16),
            pltpu.VMEM((N, N, 4, width), bf16),
            pltpu.VMEM((N, 4, width), bf16),
            pltpu.VMEM((N * N, N * 4, 1280), bf16),
            pltpu.VMEM((4, hidden, width), bf16),
            pltpu.VMEM((2, hidden, width), bf16),
            pltpu.VMEM((4 * hidden, rows), f32),
            pltpu.VMEM((rows, 2 * hidden), bf16),
            pltpu.VMEM((2, columns, width), bf16),
            pltpu.VMEM((2 * half, rows), f32),
            pltpu.VMEM((TOPK, half // 16, rows), f32),
            pltpu.VMEM((128, rows), f32),
            pltpu.VMEM((rows, 128), f32),
            pltpu.VMEM((1, rows), jnp.int32),
            stat, stat,
            pltpu.VMEM((2, 1, 128), f32),
            pltpu.VMEM((N, N, N, 1, 128), f32),
            pltpu.VMEM((N, N, N, 1, 128), f32),
            pltpu.VMEM((1, rows), f32),
            dma(4), dma(5), dma(5), dma(42), dma(42), dma(18), dma(18), dma(42), dma(42), dma(3), dma(3), dma(3), dma(3), dma(3), dma(3),
        ],
        compiler_params=pltpu.CompilerParams(collective_id=0, has_side_effects=True, vmem_limit_bytes=67043328),
        name="score",
    )(h, gain_ffn, gain_final, w_gate, w_up, w_down, head, ids, seq_ids)


def emit_kernel(x_ref, lp_ref, ln_ref, tm_ref, sq_ref):
    for n, ref in enumerate((lp_ref, ln_ref, tm_ref, sq_ref)):
        size = ref.shape[1]
        line = x_ref[pl.ds(n, 1), :]
        ref[0:1, :] = line[:, 0:size]
        ref[1:2, :] = pltpu.roll(line, 128 - size, 1)[:, 0:size]


def emit(x, own):
    f32 = jnp.float32
    small = jax.ShapeDtypeStruct((2, own), f32)
    return pl.pallas_call(
        emit_kernel, out_shape=(small, small, small, jax.ShapeDtypeStruct((2, SEQS), f32)), name="emit"
    )(x)


def body(hidden_in, gain_ffn, w_gate, w_up, w_down, gain_final, head_weight, sampled_ids, seq_ids):
    width = hidden_in.shape[-1]
    packed = score(
        hidden_in, gain_ffn.reshape(1, width), gain_final.reshape(1, width),
        w_gate.T, w_up.T, w_down, head_weight.T, sampled_ids, seq_ids,
    )
    return tuple(emit(packed, hidden_in.shape[1]))


def solution(mesh):
    split = Mesh(mesh.devices.reshape(mesh.shape["section"], N, N, N), EVERY)
    rows = P(None, EVERY)
    return jax.shard_map(
        body,
        mesh=split,
        in_specs=(P(None, EVERY, None), P(), rows, rows, P(EVERY, None), P(), rows, P(), rows),
        out_specs=(rows, rows, rows, P()),
        check_vma=False,
    )
```

```python
import functools

import jax
import jax.numpy as jnp
from jax import lax
from jax.experimental import pallas as pl
from jax.experimental.pallas import tpu as pltpu
from jax.sharding import Mesh
from jax.sharding import PartitionSpec as P

SEQS = 8
TOPK = 20
EPS = 1e-06
NEG = -3.0e38
MESH = pl.DeviceIdType.MESH
CORE = "section"
WAVES = (0, 1, 2)
AXES = ("x", "z", "y")
EVERY = (CORE,) + AXES
ORDERS = ((0, 1, 2), (1, 2, 0), (2, 0, 1))
N = 4


def pick(sel):
    return tuple(sel.get(i, slice(None)) for i in range(3))


def column_groups(width):
    tiles = width // 128
    cuts = [0, (tiles + 2) // 3, (2 * tiles + 2) // 3, tiles]
    waves = [[] for _ in WAVES]
    for q in range(3):
        tile, size = cuts[q], cuts[q + 1] - cuts[q]
        for n, wave in enumerate(waves):
            part = size // len(waves) + (1 if (n - q) % len(waves) < size % len(waves) else 0)
            wave.append((128 * tile, 128 * part))
            tile += part
    return waves


def toward(axis, k):
    name = AXES[axis]
    return {name: lax.rem(lax.axis_index(name) + k, N)}


def partner():
    return {CORE: 1 - lax.axis_index(CORE)}


def away(i, j, k):
    offsets = (i, j, k)
    return {name: lax.rem(lax.axis_index(name) + offsets[n], N) for n, name in enumerate(AXES)}


FAR = sorted(
    ((i, j, k) for i in range(N) for j in range(N) for k in range(N)),
    key=lambda at: -sum(min(v, N - v) for v in at),
)


def greet():
    barrier = pltpu.get_barrier_semaphore()
    for axis in range(3):
        for k in (1, 2, 3):
            pl.semaphore_signal(barrier, inc=1, device_id=toward(axis, k), device_id_type=MESH)
    pl.semaphore_signal(barrier, inc=1, device_id=partner(), device_id_type=MESH)


def met():
    pl.semaphore_wait(pltpu.get_barrier_semaphore(), 10)


class Mail:
    def __init__(self, send_sem, recv_sem):
        self.send_sem, self.recv_sem = send_sem, recv_sem
        self.wholes, self.places = {}, {}

    def send(self, tag, whole, src, dst, device):
        place = self.places.setdefault(tag, len(self.places))
        self.wholes[tag] = whole
        pltpu.make_async_remote_copy(
            src_ref=src,
            dst_ref=dst,
            send_sem=self.send_sem.at[place],
            recv_sem=self.recv_sem.at[place],
            device_id=device,
            device_id_type=MESH,
        ).start()

    def all_of(self, tag):
        place, whole = self.places[tag], self.wholes[tag]
        return pltpu.make_async_remote_copy(
            src_ref=whole,
            dst_ref=whole,
            send_sem=self.send_sem.at[place],
            recv_sem=self.recv_sem.at[place],
            device_id=partner(),
            device_id_type=MESH,
        )

    def received(self, tag):
        self.all_of(tag).wait_recv()

    def all_sent(self):
        for tag in self.places:
            self.all_of(tag).wait_send()

    def spread(self, src, dst, only=None):
        some = pl.ds(1, 3)
        wholes = (dst.at[some], dst.at[0, some], dst.at[0, 0, some])
        for at in FAR[:-1]:
            if only is None or only(at):
                tag = 0 if at[0] else 1 if at[1] else 2
                self.send(tag, wholes[tag], src(*at), dst.at[tuple((N - v) % N for v in at)], away(*at))

    def all_received(self):
        for tag in self.places:
            self.received(tag)


class Gather:
    def __init__(self, buf, mail, groups):
        self.buf, self.mail, self.groups = buf, mail, groups

    def each(self, s, tag, sel, along, after=None):
        for q, axes in enumerate(ORDERS):
            named = dict(zip("abc", axes))
            axis = named[along]
            if after:
                self.mail.received((s, q, after))
            rest = (slice(None), pl.ds(*self.groups[s][q]))

            def part(at):
                return self.buf.at[pick({**{named[n]: v for n, v in sel.items()}, axis: at}) + rest]

            for k in (1, 3, 2):
                self.mail.send((s, q, tag), part(pl.ds(1, 3)), part(0), part(N - k), toward(axis, k))

    def open(self, s):
        self.each(s, "a", {"b": 0, "c": 0}, "a")
        self.each(s, "b0", {"a": 0, "c": 0}, "b")
        if s == 0:
            self.each(0, "c0", {"a": 0, "b": 0}, "c")

    def relay(self):
        others = pl.ds(1, 3)
        for s in WAVES:
            self.each(s, "b1", {"a": others, "c": 0}, "b", "a")
            if s == 0:
                self.each(s, "c1", {"a": others, "b": 0}, "c")
        self.each(0, "c2", {"a": 0, "b": others}, "c", "b0")
        self.each(0, "c3", {"a": others, "b": others}, "c", "b1")
        for s in WAVES[1:]:
            self.each(s, "c0", {"a": 0, "b": 0}, "c")
            self.each(s, "c1", {"a": others, "b": 0}, "c")
            self.each(s, "c2", {"a": 0, "b": others}, "c", "b0")
            self.each(s, "c3", {"a": others, "b": others}, "c", "b1")


def gather_end(buf, out, mail, groups, s):
    for tag in ("c0", "c1", "c2", "c3"):
        for q in range(3):
            mail.received((s, q, tag))

    @pl.loop(0, N)
    def _(i):
        @pl.loop(0, N)
        def _(j):
            for k in range(N):
                for q in range(3):
                    cols = pl.ds(*groups[s][q])
                    out[i * N + j, pl.ds(4 * k, 4), cols] = buf[i, j, k, :, cols]


def rms(wide, gain):
    mean = jnp.mean(wide * wide, axis=-1, keepdims=True)
    return (wide * lax.rsqrt(mean + EPS) * gain).astype(jnp.bfloat16)


def by_tokens(weight, x, groups, s):
    rows = x.shape[0] * x.shape[1]
    total = None
    for q in range(3):
        cols = pl.ds(*groups[s][q])
        part = lax.dot_general(
            weight(cols), x[:, :, cols].reshape(rows, groups[s][q][1]), (((1,), (1,)), ((), ())),
            preferred_element_type=jnp.float32,
        )
        total = part if total is None else total + part
    return total


def order_ids(ids_ref, IDS, Q, V, own):
    Q[...] = jnp.zeros_like(Q)
    Q[0:2, :] = ids_ref[...].astype(jnp.float32)
    V[...] = Q[...].T
    size = ids_ref.shape[1]
    place = lax.broadcasted_iota(jnp.int32, (size, N**3 * 4), 1)
    row = lax.broadcasted_iota(jnp.int32, (size, N**3 * 4), 0)
    chip = jnp.zeros_like(place)
    for n, name in enumerate(AXES):
        chip = chip * N + lax.rem(lax.axis_index(name) + lax.rem(place // (4 * N ** (2 - n)), N), N)
    slot = (lax.axis_index(CORE) * N**3 + chip) * own + lax.rem(place, own)
    value = jnp.where(lax.rem(place, 4) // own == 0, V[:, 0:1], V[:, 1:2])
    IDS[...] = jnp.sum(jnp.where(row == slot, value, 0.0), axis=0, keepdims=True).astype(jnp.int32)


def sort_pairs(n):
    pairs, p = [], 1
    while p < n:
        k = p
        while k >= 1:
            for j in range(k % p, n - k, 2 * k):
                for i in range(min(k, n - j - k)):
                    if (i + j) // (2 * p) == (i + j + k) // (2 * p):
                        pairs.append((i + j, i + j + k))
            k //= 2
        p *= 2
    return pairs


def sort_down(values):
    values = list(values)
    for i, j in sort_pairs(len(values)):
        values[i], values[j] = jnp.maximum(values[i], values[j]), jnp.minimum(values[i], values[j])
    return values


def merge_down(left, right, keep=TOPK):
    left = list(left) + [False] * (keep - len(left))
    right = list(right) + [False] * (keep - len(right))

    def order(u, v):
        if u is None or v is False:
            return u, v
        if v is None or u is False:
            return v, u
        return jnp.maximum(u, v), jnp.minimum(u, v)

    line = [order(left[i], right[keep - 1 - i])[0] for i in range(keep)] + [None] * (32 - keep)
    gap = 16
    while gap:
        for i in range(32):
            if not i & gap:
                line[i], line[i + gap] = order(line[i], line[i + gap])
        gap //= 2
    return line[32 - keep :]


def row_factors(C):
    lane = lax.broadcasted_iota(jnp.int32, (1, N**3 * 4), 1)
    total = jnp.zeros((1, N**3 * 4), jnp.float32)
    for i in range(N):
        for j in range(N):
            for k in range(N):
                line = jnp.concatenate([C[i, j, k]] * (N**3 * 4 // 128), axis=1)
                total = total + jnp.where(lane // 4 == (i * N + j) * N + k, line, 0.0)
    return total


def slot_stats(LT, M, Q, V, IDS, ST, U, mail, columns):
    levels, rows = 16, LT.shape[1]
    deep = LT.shape[0] // levels
    chip = (lax.axis_index("x") * N + lax.axis_index("z")) * N + lax.axis_index("y")
    core = lax.axis_index(CORE)
    first = (core * N**3 + chip) * columns
    second = ((1 - core) * N**3 + chip) * columns
    for t in range(rows // 128):
        lanes = pl.ds(128 * t, 128)
        ids = IDS[:, lanes]

        @pl.loop(0, deep // 16)
        def _(j):
            both = []
            for side in range(2):
                at = pl.multiple_of(side * (deep // 2) + j * 8, 8)
                both.append(sort_down([LT[pl.ds(l * deep + at, 8), lanes] for l in range(levels)]))
            for l, value in enumerate(merge_down(*both)):
                M[l, pl.ds(pl.multiple_of(j * 8, 8), 8), lanes] = value

        have = deep // 16
        while have > 1:
            have //= 2

            @pl.loop(0, have)
            def _(j):
                both = []
                for side in range(2):
                    at = pl.multiple_of((side * have + j) * 8, 8)
                    both.append([M[l, pl.ds(at, 8), lanes] for l in range(TOPK)])
                for l, value in enumerate(merge_down(*both)):
                    M[l, pl.ds(pl.multiple_of(j * 8, 8), 8), lanes] = value

        top = [M[l, pl.ds(0, 8), lanes] for l in range(TOPK)]
        for shift in (4, 2, 1):
            top = merge_down(top, [pltpu.roll(v, shift, 0) for v in top])
        peak = top[0]

        def body(j, carry):
            total, hit = carry
            at = pl.multiple_of(j * 8, 8)
            value = LT[pl.ds(at, 8), lanes]
            row = lax.broadcasted_iota(jnp.int32, (8, 128), 0) + at
            late = row >= LT.shape[0] // 2
            column = jnp.where(late, row - LT.shape[0] // 2, row)
            token = column + jnp.where(late, second, first)
            same = (token == ids) & (column < columns)
            return total + jnp.exp(value - peak), hit + jnp.where(same, value, 0.0)

        zero = jnp.zeros((8, 128), jnp.float32)
        total, hit = lax.fori_loop(0, LT.shape[0] // 8, body, (zero, zero), unroll=8)
        for l in range(TOPK):
            Q[pl.ds(l, 1), lanes] = top[l][0:1]
        Q[pl.ds(TOPK, 1), lanes] = jnp.sum(total, axis=0, keepdims=True)
        Q[pl.ds(TOPK + 1, 1), lanes] = jnp.sum(hit, axis=0, keepdims=True)
        V[lanes, :] = Q[:, lanes].T
        for at in FAR:
            i, j, k = at
            if (i * N**2 + j * N + k) * 4 // 128 == t:
                to = U if at == (0, 0, 0) else ST
                to[i, j, k] = V[pl.ds(((i * N + j) * N + k) * 4, 4), :]
        mail.spread(lambda *at: ST.at[at], U, lambda at: (at[0] * N**2 + at[1] * N + at[2]) * 4 // 128 == t)


def merged(U, V, Q):
    for i in range(N):
        for j in range(N):
            for k in range(N):
                V[pl.ds(((i * N + j) * N + k) * 4, 4), :] = U[i, j, k]
    Q[...] = V[...].T

    def line(l):
        return [Q[pl.ds(l, 1), pl.ds(128 * t, 128)] for t in range(2)]

    lists = [line(l) for l in range(TOPK)]
    top = merge_down([v[0] for v in lists], [v[1] for v in lists])
    for shift in (64, 32, 16, 8, 4):
        top = merge_down(top, [pltpu.roll(v, shift, 1) for v in top])
    peak = top[0]
    sums, hits = line(TOPK), line(TOPK + 1)
    total = sum(s * jnp.exp(v - peak) for s, v in zip(sums, lists[0]))
    hit = hits[0] + hits[1]
    for shift in (64, 32, 16, 8, 4):
        total = total + pltpu.roll(total, shift, 1)
        hit = hit + pltpu.roll(hit, shift, 1)
    log_norm = peak + jnp.log(total)
    mass = sum(jnp.exp(v - log_norm) for v in top)
    return hit - log_norm, log_norm, mass


def by_sequence(logprob, sid_ref):
    lane = lax.broadcasted_iota(jnp.int32, (1, 128), 1)
    turned = [logprob] + [pltpu.roll(logprob, j, 1) for j in (1, 2, 3)]
    part = jnp.zeros((1, 128), jnp.float32)
    for t in range(4):
        spread = turned[0]
        for j in (1, 2, 3):
            spread = jnp.where(lax.rem(lane - t + 4, 4) == j, turned[j], spread)
        mine = (lane // SEQS == t // 2) & (lax.rem(lane, SEQS) == sid_ref[t // 2, t % 2])
        part = part + jnp.where(mine, spread, 0.0)
    return part


def score_kernel(
    h_ref, gf_ref, gl_ref, wg_ref, wu_ref, wd_ref, hw_ref, ids_ref, sid_ref,
    out_ref,
    HS, G, X, S, R1, R2, R3, T1, T2, PB, W, WD, Y, ACT, HB, LT, M, Q, V, IDS, ST, U, A, B, C, FS,
    own_s, swap_s, swap_r, g_s, g_r, r_s, r_r, g2_s, g2_r, a_s, a_r, q_s, q_r, c_s, c_r,
):
    width = h_ref.shape[-1]
    groups = column_groups(width)
    rows = N**3 * 4
    hidden = W.shape[1]
    columns = HB.shape[1]
    loads = []
    for n, (src, dst) in enumerate(((wg_ref, W.at[0]), (wu_ref, W.at[1]), (wd_ref, WD.at[0]))):
        copy = pltpu.make_async_copy(src, dst, own_s.at[n])
        copy.start()
        loads.append(copy)
    greet()
    own = h_ref.shape[1]
    for m in range(h_ref.shape[0]):
        HS[pl.ds(m * own, own), :] = h_ref[m].astype(jnp.float32)
    G[0, 0, 0] = rms(HS[...], gf_ref[...])
    met()
    mail = Mail(g_s, g_r)
    swap = Mail(swap_s, swap_r)
    for tag, src, dst in (("g", wg_ref, W.at[2]), ("u", wu_ref, W.at[3]), ("d", wd_ref, WD.at[1])):
        swap.send(tag, dst, src, dst, partner())
    gather = Gather(G, mail, groups)
    for s in WAVES:
        gather.open(s)
    gather.relay()
    order_ids(ids_ref, IDS, Q, V, own)
    for copy in loads[:2]:
        copy.wait()
    for tag in ("g", "u"):
        swap.received(tag)
    for s in WAVES:
        gather_end(G, X, mail, groups, s)
        part = by_tokens(lambda cols: W[:, :, cols].reshape(4 * hidden, cols.size), X, groups, s)
        Y[...] = part if s == 0 else Y[...] + part
    loads[2].wait()
    swap.received("d")
    swap.send("h", HB.at[1], hw_ref, HB.at[1], partner())
    own_head = pltpu.make_async_copy(hw_ref, HB.at[0], own_s.at[3])
    own_head.start()
    acts = []
    for p in range(2):
        gate, up = Y[pl.ds(2 * p * hidden, hidden), :], Y[pl.ds((2 * p + 1) * hidden, hidden), :]
        acts.append(gate / (1.0 + jnp.exp(-gate)) * up)
    ACT[...] = jnp.concatenate(acts, axis=0).T.astype(jnp.bfloat16)
    mail.all_sent()

    red = Mail(r_s, r_r)

    def down(at, size):
        cols = pl.ds(at, size)
        part = jnp.dot(ACT[...], WD[:, :, cols].reshape(2 * hidden, size), preferred_element_type=jnp.float32)
        PB[:, :, pl.ds(0, size)] = part.astype(jnp.bfloat16).reshape(N * N, N * 4, size)
        for i in range(N):
            for j in range(N):
                for k in range(N):
                    S[i, j, k, :, cols] = PB[i * N + j, pl.ds(4 * k, 4), pl.ds(0, size)]

    every = [(s, q, pl.ds(*groups[s][q])) + ORDERS[q] for s in WAVES for q in range(3)]
    for s, q, cols, a, b, c in every:
        start, size = groups[s][q]

        down(start, size)
        rest = (slice(None), cols)
        for k in (2, 1, 3):
            whole = R1.at[:, :, :, :, cols]
            red.send((s, q, 1), whole, S.at[pick({c: k}) + rest], R1.at[k - 1, :, :, :, cols], toward(c, k))
    for s, q, cols, a, b, c in every:
        red.received((s, q, 1))

        @pl.loop(0, N)
        def _(i):
            @pl.loop(0, N)
            def _(j):
                left = [i, j]
                sel = {ax: left.pop(0) for ax in range(3) if ax != c}
                sel[c] = 0
                total = S[pick(sel) + (slice(None), cols)].astype(jnp.float32)
                for k in range(3):
                    total += R1[k, i, j, :, cols].astype(jnp.float32)
                T1[i, j, :, cols] = total.astype(jnp.bfloat16)

        first = min(a, b)
        for k in (2, 1, 3):
            src = T1.at[k, :, :, cols] if b == first else T1.at[:, k, :, cols]
            red.send((s, q, 2), R2.at[:, :, :, cols], src, R2.at[k - 1, :, :, cols], toward(b, k))
    for s, q, cols, a, b, c in every:
        red.received((s, q, 2))
        first = min(a, b)
        for i in range(N):
            total = (T1[0, i, :, cols] if b == first else T1[i, 0, :, cols]).astype(jnp.float32)
            for k in range(3):
                total += R2[k, i, :, cols].astype(jnp.float32)
            T2[i, :, cols] = total.astype(jnp.bfloat16)
        for k in (2, 1, 3):
            red.send((s, q, 3), R3.at[:, :, cols], T2.at[k, :, cols], R3.at[k - 1, :, cols], toward(a, k))
    mail2 = Mail(g2_s, g2_r)
    gather = Gather(G, mail2, groups)
    squares = jnp.zeros((4, 1), jnp.float32)
    for s in WAVES:
        for q in range(3):
            cols = pl.ds(*groups[s][q])
            red.received((s, q, 3))
            total = T2[0, :, cols].astype(jnp.float32)
            for k in range(3):
                total += R3[k, :, cols].astype(jnp.float32)
            residual = (HS[:, cols] + total).astype(jnp.bfloat16).astype(jnp.float32)
            squares += jnp.sum(residual * residual, axis=-1, keepdims=True)
            G[0, 0, 0, :, cols] = (residual * gl_ref[:, cols]).astype(jnp.bfloat16)
        gather.open(s)
    factor = jnp.broadcast_to(lax.rsqrt(squares / width + EPS), (4, 128))
    turn = lax.rem(lax.broadcasted_iota(jnp.int32, (4, 128), 1), 4) == lax.broadcasted_iota(jnp.int32, (4, 128), 0)
    C[0, 0, 0] = jnp.sum(jnp.where(turn, factor, 0.0), axis=0, keepdims=True)
    gather.relay()
    scales = Mail(c_s, c_r)
    scales.spread(lambda *at: C.at[0, 0, 0], C)
    swap.received("h")
    own_head.wait()
    half, tall = LT.shape[0] // 2, 512
    for s in WAVES:
        gather_end(G, X, mail2, groups, s)
        if s == WAVES[-1]:
            scales.all_received()
            FS[...] = row_factors(C)
        for p in range(2):
            if s == 0:
                LT[pl.ds(p * half + columns // 8 * 8, half - columns // 8 * 8), :] = jnp.full(
                    (half - columns // 8 * 8, rows), NEG, jnp.float32
                )

            def logits(at, size):
                part = by_tokens(lambda cols: HB[p, pl.ds(at, size), cols], X, groups, s)
                to = pl.ds(p * half + at, size)
                total = part if s == 0 else LT[to, :] + part
                LT[to, :] = total * FS[...] if s == WAVES[-1] else total

            for at in range(0, columns, tall):
                logits(at, min(tall, columns - at))

    stats = Mail(a_s, a_r)
    slot_stats(LT, M, Q, V, IDS, ST, U, stats, columns)
    stats.all_received()
    logprob, log_norm, mass = merged(U, V, Q)

    A[0] = by_sequence(logprob, sid_ref)
    seq = Mail(q_s, q_r)
    swap.send("s", A.at[1], A.at[0], A.at[1], partner())
    swap.received("s")
    B[0, 0, 0] = A[0] + A[1]
    seq.spread(lambda *at: B.at[0, 0, 0], B)
    seq.all_received()

    def joined(values):
        return (values[0] + values[2]) + (values[1] + values[3])

    both = joined([joined([joined([B[i, j, k] for i in range(N)]) for j in range(N)]) for k in range(N)])
    for n, value in enumerate((logprob, log_norm, mass, both)):
        out_ref[pl.ds(n, 1), :] = value
    out_ref[4:8, :] = jnp.zeros((4, 128), jnp.float32)
    for m in (swap, red, mail2, scales, stats, seq):
        m.all_sent()


def score(h, gain_ffn, gain_final, w_gate, w_up, w_down, head, ids, seq_ids):
    hidden, width = w_gate.shape
    columns = head.shape[0]
    half = -(-columns // 256) * 256
    rows = N**3 * 4
    bf16, f32 = jnp.bfloat16, jnp.float32
    vmem, anywhere = pl.BlockSpec(memory_space=pltpu.VMEM), pl.BlockSpec(memory_space=pl.ANY)
    dma = lambda n: pltpu.SemaphoreType.DMA((n,))
    stat = pltpu.VMEM((N, N, N, 4, 128), f32)
    return pl.pallas_call(
        score_kernel,
        out_shape=jax.ShapeDtypeStruct((8, 128), f32),
        in_specs=[vmem, vmem, vmem, anywhere, anywhere, anywhere, anywhere, vmem, pl.BlockSpec(memory_space=pltpu.SMEM)],
        out_specs=vmem,
        scratch_shapes=[
            pltpu.VMEM((4, width), f32),
            pltpu.VMEM((N, N, N, 4, width), bf16),
            pltpu.VMEM((N * N, N * 4, width), bf16),
            pltpu.VMEM((N, N, N, 4, width), bf16),
            pltpu.VMEM((3, N, N, 4, width), bf16),
            pltpu.VMEM((3, N, 4, width), bf16),
            pltpu.VMEM((3, 4, width), bf16),
            pltpu.VMEM((N, N, 4, width), bf16),
            pltpu.VMEM((N, 4, width), bf16),
            pltpu.VMEM((N * N, N * 4, 1280), bf16),
            pltpu.VMEM((4, hidden, width), bf16),
            pltpu.VMEM((2, hidden, width), bf16),
            pltpu.VMEM((4 * hidden, rows), f32),
            pltpu.VMEM((rows, 2 * hidden), bf16),
            pltpu.VMEM((2, columns, width), bf16),
            pltpu.VMEM((2 * half, rows), f32),
            pltpu.VMEM((TOPK, half // 16, rows), f32),
            pltpu.VMEM((128, rows), f32),
            pltpu.VMEM((rows, 128), f32),
            pltpu.VMEM((1, rows), jnp.int32),
            stat, stat,
            pltpu.VMEM((2, 1, 128), f32),
            pltpu.VMEM((N, N, N, 1, 128), f32),
            pltpu.VMEM((N, N, N, 1, 128), f32),
            pltpu.VMEM((1, rows), f32),
            dma(4), dma(5), dma(5), dma(21 * len(WAVES)), dma(21 * len(WAVES)), dma(9 * len(WAVES)), dma(9 * len(WAVES)), dma(21 * len(WAVES)), dma(21 * len(WAVES)), dma(3), dma(3), dma(3), dma(3), dma(3), dma(3),
        ],
        compiler_params=pltpu.CompilerParams(collective_id=0, has_side_effects=True, vmem_limit_bytes=67043328),
        name="score",
    )(h, gain_ffn, gain_final, w_gate, w_up, w_down, head, ids, seq_ids)


def emit_kernel(x_ref, lp_ref, ln_ref, tm_ref, sq_ref):
    for n, ref in enumerate((lp_ref, ln_ref, tm_ref, sq_ref)):
        size = ref.shape[1]
        line = x_ref[pl.ds(n, 1), :]
        ref[0:1, :] = line[:, 0:size]
        ref[1:2, :] = pltpu.roll(line, 128 - size, 1)[:, 0:size]


def emit(x, own):
    f32 = jnp.float32
    small = jax.ShapeDtypeStruct((2, own), f32)
    return pl.pallas_call(
        emit_kernel, out_shape=(small, small, small, jax.ShapeDtypeStruct((2, SEQS), f32)), name="emit"
    )(x)


def body(hidden_in, gain_ffn, w_gate, w_up, w_down, gain_final, head_weight, sampled_ids, seq_ids):
    width = hidden_in.shape[-1]
    packed = score(
        hidden_in, gain_ffn.reshape(1, width), gain_final.reshape(1, width),
        w_gate.T, w_up.T, w_down, head_weight.T, sampled_ids, seq_ids,
    )
    return tuple(emit(packed, hidden_in.shape[1]))


def solution(mesh):
    split = Mesh(mesh.devices.reshape(mesh.shape["section"], N, N, N), EVERY)
    rows = P(None, EVERY)
    return jax.shard_map(
        body,
        mesh=split,
        in_specs=(P(None, EVERY, None), P(), rows, rows, P(EVERY, None), P(), rows, P(), rows),
        out_specs=(rows, rows, rows, P()),
        check_vma=False,
    )
```
